256 devices in a mesh: grp: 4 (over z_hi), gx: 4 (over x), gy: 16 (over z_lo, y, core).
Axes of the slice: x: 4, y: 4, z: 8 (z_hi: 4, z_lo: 2; z = z_hi * 2 + z_lo), core: 2. Of those that a mesh axis runs over, the one named last changes fastest.
Arguments:
- state: float32 [4, 5, 16, 64, 2048], P('grp', None, None, 'gx', 'gy'), as said below
- view_dir: int32 [64], P('gx'), may hold values from 0 to 1
Outputs:
- new_state: float32 [4, 5, 16, 64, 2048], P('grp', None, None, 'gx', 'gy')
- side_view: float32 [4, 64, 3, 16], P('grp', 'gx', None, 'gy')
- occupancy_fine: bfloat16 [4, 12, 16, 512], P('grp', None, 'gx', 'gy')
- occupancy_coarse: bfloat16 [4, 3, 4, 128], P('grp', None, 'gx', 'gy')
The draws below stay inside these ranges and needn't reach their ends.
Inputs may be any that keep to these rules, and one draw needn't show every extreme that they name: `state`: in every cell the density is positive and the pressure 0.4 (field 4 - (field 1 squared + field 2 squared + field 3 squared) / (2 field 0)) is positive.
All inputs are finite; a program needn't handle non-finite values.
Results may differ from the reference program's by a relative error of at most 0.0035.
The reference program's roundings to bfloat16 on the way count: a program that leaves them out, or rounds other values in their place, can miss the bound.
Values may be sent and summed in bfloat16 or wider, within the bound.
A program may use at most 64 MiB of HBM per device.

```python
import jax
import jax.numpy as jnp
from jax import lax

FIELDS = 5
CX = 16
LAYER_DEPTH_UP = 16
SLABS = 3
GRID_WIDTH_EAST = 64
GRID_WIDTH_NORTH = 2048
N_GRP = 4
N_GX = 4


def draw_state(key, part):
    random_seed_parts = jax.random.split(key, 3)
    planes = N_GRP * LAYER_DEPTH_UP
    depth_pos = (jnp.arange(planes, dtype=jnp.float32) / (planes - 1.0)).reshape(N_GRP, 1, LAYER_DEPTH_UP, 1, 1)
    row_pos = (jnp.arange(GRID_WIDTH_EAST, dtype=jnp.float32) / (GRID_WIDTH_EAST - 1.0)).reshape(1, 1, 1, GRID_WIDTH_EAST, 1)
    col_pos = (jnp.arange(GRID_WIDTH_NORTH, dtype=jnp.float32) / (GRID_WIDTH_NORTH - 1.0)).reshape(1, 1, 1, 1, GRID_WIDTH_NORTH)
    along_x = jnp.array([0.0, 1.0, 0.0], jnp.float32).reshape(1, 3, 1, 1, 1)
    ramp = 0.5 + (depth_pos + row_pos + col_pos) / 3.0
    fluid_rho_field = jnp.exp(0.5 * jnp.clip(jax.random.normal(random_seed_parts[0], (N_GRP, 1, LAYER_DEPTH_UP, GRID_WIDTH_EAST, GRID_WIDTH_NORTH), jnp.float32), -3.2, 3.2))
    spread = jnp.clip(jax.random.normal(random_seed_parts[1], (N_GRP, 3, LAYER_DEPTH_UP, GRID_WIDTH_EAST, GRID_WIDTH_NORTH), jnp.float32), -3.0, 3.0)
    velocity = ramp * (6.0 * along_x + (0.6 + 0.4 * along_x) * spread)
    fluid_thermal_field = jax.random.uniform(random_seed_parts[2], (N_GRP, 1, LAYER_DEPTH_UP, GRID_WIDTH_EAST, GRID_WIDTH_NORTH), jnp.float32, 0.5, 1.0)
    fluid_stress_field = fluid_rho_field * fluid_thermal_field
    momentum = fluid_rho_field * velocity
    energy = fluid_stress_field / 0.4 + 0.5 * fluid_rho_field * jnp.sum(velocity * velocity, axis=1, keepdims=True)
    return jnp.concatenate([fluid_rho_field, momentum, energy], axis=1)


def with_ends(drawn, own_key, least, top_value):
    longest = drawn.shape.index(max(drawn.shape))
    spots = []
    for shift in (0, 1):
        where = [jax.random.randint(jax.random.fold_in(own_key, axis), (), 0, length) for axis, length in enumerate(drawn.shape)]
        where[longest] = (where[longest] + shift) % drawn.shape[longest]
        spots.append(tuple(where))
    return drawn.at[spots[0]].set(least).at[spots[1]].set(top_value)


def setup_inputs(seed: int = 0) -> dict:
    arg_keys = jax.random.split(jax.random.key(seed), 3)
    return {
        "state": draw_state(jax.random.fold_in(arg_keys[2], 71), 0),
        "view_dir": with_ends(jax.random.randint(arg_keys[1], (GRID_WIDTH_EAST,), 0, 2), jax.random.fold_in(arg_keys[1], 1), 0, 1).astype(jnp.int32),
    }


gamma_gas = 1.4
courant = 0.8

def minmod(backward, forward):
    return jnp.maximum(0.0, jnp.minimum(backward, forward)) + jnp.minimum(0.0, jnp.maximum(backward, forward))

def primitive(fields):
    fluid_rho_field = fields[0]
    velocity = fields[1:4] / fluid_rho_field
    fluid_stress_field = (gamma_gas - 1.0) * (fields[4] - 0.5 * lax.optimization_barrier(jnp.sum(fields[1:4] * velocity, axis=0)))
    return jnp.concatenate([fluid_rho_field[None], velocity, fluid_stress_field[None]], axis=0)

def conserved(states):
    fluid_rho_field = states[0]
    momentum = states[1:4] * fluid_rho_field
    energy = states[4] / (gamma_gas - 1.0) + 0.5 * lax.optimization_barrier(jnp.sum(momentum * states[1:4], axis=0))
    return jnp.concatenate([fluid_rho_field[None], momentum, energy[None]], axis=0)

def physical_flux(states, fields, normal):
    normal_speed = states[normal]
    fluid_stress_field = states[4]
    extra = jnp.zeros_like(fields).at[normal].set(fluid_stress_field).at[4].set(fluid_stress_field * normal_speed)
    return fields * normal_speed + extra

def sound_reach(states, normal):
    return jnp.abs(states[normal]) + jnp.sqrt(gamma_gas * states[4] / states[0])

def slice_along(values, start, length, direction):
    return lax.slice_in_dim(values, start, start + length, axis=direction)

def divergence(padded, direction):
    length = padded.shape[direction] - 4
    states = primitive(padded)
    differences = slice_along(states, 1, length + 3, direction) - slice_along(states, 0, length + 3, direction)
    slopes = minmod(slice_along(differences, 0, length + 2, direction), slice_along(differences, 1, length + 2, direction))
    lower_state = slice_along(states, 1, length + 1, direction) + 0.5 * slice_along(slopes, 0, length + 1, direction)
    upper_state = slice_along(states, 2, length + 1, direction) - 0.5 * slice_along(slopes, 1, length + 1, direction)
    lower_fields = conserved(lower_state)
    upper_fields = conserved(upper_state)
    wave_speed = jnp.maximum(sound_reach(lower_state, direction), sound_reach(upper_state, direction))
    face_flux = 0.5 * (physical_flux(lower_state, lower_fields, direction) + physical_flux(upper_state, upper_fields, direction)) - 0.5 * wave_speed * (upper_fields - lower_fields)
    return slice_along(face_flux, 1, length, direction) - slice_along(face_flux, 0, length, direction)

def advance_block(padded, time_step):
    inner = padded[:, 2:-2, 2:-2, 2:-2]
    change = divergence(padded[:, :, 2:-2, 2:-2], 1)
    change = change + divergence(padded[:, 2:-2, :, 2:-2], 2)
    change = change + divergence(padded[:, 2:-2, 2:-2, :], 3)
    return inner - time_step * change

def max_speed(fields):
    states = primitive(fields)
    return jnp.max(lax.optimization_barrier(jnp.sum(jnp.abs(states[1:4]), axis=0)) + 3.0 * jnp.sqrt(gamma_gas * states[4] / states[0]))

def pool_once(volume):
    num_planes, num_rows, num_cols = volume.shape
    return lax.optimization_barrier(jnp.max(volume.reshape(num_planes // 2, 2, num_rows // 2, 2, num_cols // 2, 2), axis=(1, 3, 5)))

def project(volume, attenuation):
    return lax.optimization_barrier(jnp.max(volume.astype(jnp.float32) * attenuation[None], axis=2))

def reference(state, view_dir):
    speeds = lax.map(max_speed, state)
    time_step = courant / jnp.max(speeds)

    def advance_slab(slab):
        below = lax.dynamic_index_in_dim(state, (slab + N_GRP - 1) % N_GRP, 0, keepdims=False)[:, LAYER_DEPTH_UP - 2:]
        middle = lax.dynamic_index_in_dim(state, slab, 0, keepdims=False)
        above = lax.dynamic_index_in_dim(state, (slab + 1) % N_GRP, 0, keepdims=False)[:, :2]
        column = jnp.concatenate([below, middle, above], axis=1)
        padded = jnp.pad(column, ((0, 0), (0, 0), (2, 2), (2, 2)), mode='wrap')

        def advance_columns(start):
            piece = lax.dynamic_slice_in_dim(padded, start, CX + 4, 2)
            return advance_block(piece, time_step)
        blocks = lax.map(advance_columns, jnp.arange(N_GX, dtype=jnp.int32) * CX)
        return jnp.moveaxis(blocks, 0, 2).reshape(FIELDS, LAYER_DEPTH_UP, GRID_WIDTH_EAST, GRID_WIDTH_NORTH)
    new_slabs = lax.map(advance_slab, jnp.arange(SLABS, dtype=jnp.int32))
    new_state = jnp.concatenate([new_slabs, state[SLABS:]], axis=0)
    snapshot = new_slabs[:, 0].astype(jnp.bfloat16)
    fraction = jnp.arange(GRID_WIDTH_NORTH, dtype=jnp.int32).astype(jnp.float32) / jnp.float32(GRID_WIDTH_NORTH - 1)
    toward = jnp.exp(-fraction)
    away_side = jnp.exp(-(1.0 - fraction))
    attenuation = jnp.where(view_dir[:, None] == 0, toward[None, :], away_side[None, :])
    views = lax.map(lambda volume: project(volume, attenuation), snapshot)
    view = jnp.transpose(views, (2, 0, 1))
    side_view = jnp.concatenate([jnp.zeros((SLABS, GRID_WIDTH_EAST, SLABS, LAYER_DEPTH_UP), jnp.float32), view[None]], axis=0)
    column = snapshot.reshape(SLABS * LAYER_DEPTH_UP, GRID_WIDTH_EAST, GRID_WIDTH_NORTH)
    level_two = pool_once(pool_once(column))
    level_four = pool_once(pool_once(level_two))
    occupancy_fine = jnp.concatenate([jnp.zeros((SLABS,) + level_two.shape, jnp.bfloat16), level_two[None]], axis=0)
    occupancy_coarse = jnp.concatenate([jnp.zeros((SLABS,) + level_four.shape, jnp.bfloat16), level_four[None]], axis=0)
    return (new_state, side_view, occupancy_fine, occupancy_coarse)
```

```python
import jax
import jax.numpy as jnp
from jax import lax
from jax.experimental import pallas as pl
from jax.experimental.pallas import tpu as pltpu
from jax.sharding import PartitionSpec as P

F32 = jnp.float32
BF16 = jnp.bfloat16
MESH = pl.DeviceIdType.MESH

NF = 5
NZ = 16
NX = 16
NY = 128
N_GRP, N_GX, N_GY = 4, 4, 16
SLABS = 3
N_Z = 8
N_PLANE = 32
WZ = NZ + 4
WX = 32


def z_partner(k):
    g, x, y = lax.axis_index("grp"), lax.axis_index("gx"), lax.axis_index("gy")
    z = lax.rem(g * 2 + y // 8 + k, N_Z)
    return {"grp": z // 2, "gx": x, "gy": lax.rem(z, 2) * 8 + lax.rem(y, 8)}


def plane_partner(k):
    g, x, y = lax.axis_index("grp"), lax.axis_index("gx"), lax.axis_index("gy")
    i = lax.rem(x * 8 + lax.rem(y, 8) + k, N_PLANE)
    return {"grp": g, "gx": i // 8, "gy": (y // 8) * 8 + lax.rem(i, 8)}


def shifted(axis, step):
    place = {a: lax.axis_index(a) for a in ("grp", "gx", "gy")}
    count = {"grp": N_GRP, "gx": N_GX, "gy": N_GY}[axis]
    place[axis] = lax.rem(place[axis] + step + count, count)
    return place


def side(state, d):
    rho, p = state[0], state[4]
    v = state[1:4]
    m = [rho * a for a in v]
    energy = 2.5 * p + 0.5 * (m[0] * v[0] + m[1] * v[1] + m[2] * v[2])
    vd = state[d]
    fields = [rho, *m, energy]
    flux = [m[d - 1], m[0] * vd, m[1] * vd, m[2] * vd, (energy + p) * vd]
    flux[d] = flux[d] + p
    return fields, flux, jnp.abs(vd) + jnp.sqrt(1.4 * p / rho)


def face(q0, q1, q2, q3, d):
    low, up = [], []
    for a0, a1, a2, a3 in zip(q0, q1, q2, q3):
        a, b, c = a1 - a0, a2 - a1, a3 - a2
        left = jnp.maximum(jnp.minimum(a, b), jnp.minimum(jnp.maximum(a, b), 0.0))
        right = jnp.maximum(jnp.minimum(b, c), jnp.minimum(jnp.maximum(b, c), 0.0))
        low.append(a1 + 0.5 * left)
        up.append(a2 - 0.5 * right)
    ul, fl, rl = side(low, d)
    uu, fu, ru = side(up, d)
    wave = jnp.maximum(rl, ru)
    return [(a + b) - wave * (e - c) for a, b, c, e in zip(fl, fu, ul, uu)]


def kernel(
    state_ref, dir_ref, new_ref, view_ref, fine_ref, coarse_ref,
    S, W, CH, FX, FZ, NEW, SN, PK, GY, VT, LH, SO,
    send_z, send_x, send_y, recv_z, recv_x, recv_y,
    max0, max1, max1v, max2, recv_v, recv_o,
    in_sem, out_sem, hs_sem, hr_sem, ms_sem, mr_sem, vs_sem, vr_sem, os_sem, or_sem,
):
    g, gy = lax.axis_index("grp"), lax.axis_index("gy")
    is_viz = g == SLABS
    load = pltpu.make_async_copy(state_ref, S, in_sem)
    load.start()

    z_parts = [z_partner(k) for k in range(1, N_Z)]
    p_parts = [plane_partner(k) for k in range(1, N_PLANE)]
    y_up, y_down = shifted("gy", 1), shifted("gy", -1)
    barrier = pltpu.get_barrier_semaphore()
    greeted = z_parts + p_parts + [y_up, y_down]
    for part in greeted:
        pl.semaphore_signal(barrier, inc=1, device_id=part, device_id_type=MESH)

    lane = lax.broadcasted_iota(jnp.int32, (8, NY), 1)
    row16 = lax.broadcasted_iota(jnp.int32, (NX, NY), 0)
    lane16 = lax.broadcasted_iota(jnp.int32, (NX, NY), 1)
    W2 = W.reshape(NF * WZ * WX, NY)

    load.wait()

    def prims(z, carry):
        top, packed = carry[0], list(carry[1:])
        here = lax.shift_right_logical(lane, 2) == z
        for t in range(2):
            rows = slice(8 * t, 8 * t + 8)
            f = [S[0, i, z, rows, :] for i in range(NF)]
            inv = 1.0 / f[0]
            v = [a * inv for a in f[1:4]]
            p = 0.4 * (f[4] - 0.5 * (f[1] * v[0] + f[2] * v[1] + f[3] * v[2]))
            top = jnp.maximum(
                top,
                jnp.abs(v[0]) + jnp.abs(v[1]) + jnp.abs(v[2]) + 3.0 * jnp.sqrt(1.4 * p * inv),
            )
            for i, q in enumerate([f[0], *v, p]):
                W[i * WZ + 2 + z, 8 + 8 * t : 16 + 8 * t, :] = q
                packed[2 * i + t] = jnp.where(here, pltpu.roll(q, 4 * z + 2, 1), packed[2 * i + t])
        return (top, *packed)

    zero = jnp.zeros((8, NY), F32)
    carry = lax.fori_loop(0, NZ, prims, (zero,) + (zero,) * 10)
    max0[0] = jnp.max(carry[0], axis=0, keepdims=True)
    for i in range(NF):
        PK[i] = jnp.concatenate([carry[1 + 2 * i], carry[2 + 2 * i]], axis=0)
        send_y[i] = PK[i].astype(BF16)
        for r in range(2):
            send_z[0, i, r] = W[i * WZ + NZ + r, 8:24, :].astype(BF16)
            send_z[1, i, r] = W[i * WZ + 2 + r, 8:24, :].astype(BF16)
            for way, row in ((0, 22 + r), (1, 8 + r)):
                halves = [
                    W2[pl.ds((i * WZ + 2 + 8 * h) * WX + row, 8, stride=WX), :] for h in range(2)
                ]
                send_x[way, i, r] = jnp.concatenate(halves, axis=0).astype(BF16)

    pl.semaphore_wait(barrier, len(greeted))

    def remote(src, dst, ssem, rsem, part):
        return pltpu.make_async_remote_copy(
            src_ref=src, dst_ref=dst, send_sem=ssem, recv_sem=rsem, device_id=part, device_id_type=MESH
        )

    for k, part in enumerate(z_parts):
        remote(max0.at[0], max1.at[k], ms_sem.at[0], mr_sem.at[0], part).start()
    halo = []
    for way in range(2):
        step = 1 - 2 * way
        halo.append(
            remote(send_y, recv_y.at[way], hs_sem.at[way], hr_sem.at[way], (y_up, y_down)[way])
        )
    for way in range(2):
        step = 1 - 2 * way
        halo.append(
            remote(
                send_x.at[way], recv_x.at[way], hs_sem.at[2 + way], hr_sem.at[2 + way], shifted("gx", step)
            )
        )
    for way in range(2):
        step = 1 - 2 * way
        halo.append(
            remote(
                send_z.at[way], recv_z.at[way], hs_sem.at[4 + way], hr_sem.at[4 + way], shifted("grp", step)
            )
        )
    for copy in halo:
        copy.start()

    def z_face(p, _):
        for t in range(2):
            rows = slice(8 + 8 * t, 16 + 8 * t)
            q = [[W[i * WZ + p + j, rows, :] for i in range(NF)] for j in range(4)]
            for i, a in enumerate(face(*q, 1)):
                FZ[p, i, 8 * t : 8 * t + 8, :] = a
        return 0

    lax.fori_loop(2, NZ - 1, z_face, 0)

    halo[0].wait()
    halo[1].wait()
    for t in range(2):
        rows = slice(8 * t, 8 * t + 8)
        q = [[], [], [], []]
        for i in range(NF):
            mine = PK[i, rows, :]
            other = recv_y[1, i, :, :].astype(F32)[rows]
            q[0].append(mine)
            q[1].append(pltpu.roll(mine, NY - 1, 1))
            q[2].append(pltpu.roll(other, NY - 2, 1))
            q[3].append(pltpu.roll(other, NY - 3, 1))
        for i, a in enumerate(face(*q, 3)):
            GY[i, rows, :] = a

    def y_pass(z, _):
        for t in range(2):
            rows = slice(8 * t, 8 * t + 8)
            q = [[], [], [], []]
            for i in range(NF):
                own = W[i * WZ + 2 + z, 8 + 8 * t : 16 + 8 * t, :]
                low = pltpu.roll(recv_y[0, i, :, :].astype(F32)[rows], lax.rem(NY - 4 * z, NY), 1)
                high = pltpu.roll(recv_y[1, i, :, :].astype(F32)[rows], 125 - 4 * z, 1)
                q[0].append(jnp.where(lane < 2, low, pltpu.roll(own, 2, 1)))
                q[1].append(jnp.where(lane < 1, pltpu.roll(low, NY - 1, 1), pltpu.roll(own, 1, 1)))
                q[2].append(own)
                q[3].append(jnp.where(lane == NY - 1, high, pltpu.roll(own, NY - 1, 1)))
            for i, a in enumerate(face(*q, 3)):
                end = pltpu.roll(GY[i, rows, :], 127 - 4 * z, 1)
                above = jnp.where(lane == NY - 1, end, pltpu.roll(a, NY - 1, 1))
                CH[i, z, rows, :] = above - a
        return 0

    lax.fori_loop(0, NZ, y_pass, 0)

    def landed(dst, sem):
        remote(dst, dst, ms_sem.at[2], sem, y_up).wait_recv()

    def left(src, sem):
        remote(src, src, sem, mr_sem.at[2], y_up).wait_send()

    landed(max1, mr_sem.at[0])
    left(max1, ms_sem.at[0])
    top = max0[0]
    for k in range(N_Z - 1):
        top = jnp.maximum(top, max1[k])
    max1v[0] = top
    for k, part in enumerate(p_parts):
        remote(max1v.at[0], max2.at[k], ms_sem.at[1], mr_sem.at[1], part).start()

    halo[2].wait()
    halo[3].wait()
    for way, row in ((0, 6), (1, 24)):
        for i in range(NF):
            for r in range(2):
                rows = recv_x[way, i, r].astype(F32)
                for h in range(2):
                    W2[pl.ds((i * WZ + 2 + 8 * h) * WX + row + r, 8, stride=WX), :] = rows[8 * h : 8 * h + 8]
    FX2 = FX.reshape(NF * NZ * 24, NY)
    for h in range(2):
        q = [
            [W2[pl.ds((i * WZ + 2 + 8 * h) * WX + 22 + j, 8, stride=WX), :] for i in range(NF)]
            for j in range(4)
        ]
        for i, a in enumerate(face(*q, 2)):
            FX2[pl.ds((i * NZ + 8 * h) * 24 + 16, 8, stride=24), :] = a

    def x_pass(z, _):
        for t in range(2):
            q = [
                [W[i * WZ + 2 + z, 6 + j + 8 * t : 14 + j + 8 * t, :] for i in range(NF)] for j in range(4)
            ]
            for i, a in enumerate(face(*q, 2)):
                FX[i * NZ + z, 8 * t : 8 * t + 8, :] = a
        for t in range(2):
            rows = slice(8 * t, 8 * t + 8)
            for i in range(NF):
                CH[i, z, rows, :] = CH[i, z, rows, :] + (
                    FX[i * NZ + z, 8 * t + 1 : 8 * t + 9, :] - FX[i * NZ + z, rows, :]
                )
        return 0

    lax.fori_loop(0, NZ, x_pass, 0)

    halo[4].wait()
    halo[5].wait()
    for i in range(NF):
        for r in range(2):
            W[i * WZ + r, 8:24, :] = recv_z[0, i, r].astype(F32)
            W[i * WZ + 2 + NZ + r, 8:24, :] = recv_z[1, i, r].astype(F32)
    lax.fori_loop(0, 2, z_face, 0)
    lax.fori_loop(NZ - 1, NZ + 1, z_face, 0)

    def gather_change(z, _):
        for i in range(NF):
            CH[i, z] = CH[i, z] + (FZ[z + 1, i] - FZ[z, i])
        return 0

    lax.fori_loop(0, NZ, gather_change, 0)

    facing = jnp.zeros((NX, NY), jnp.int32)
    for x in range(NX):
        facing = jnp.where(row16 == x, dir_ref[x], facing)
    fraction = (gy * NY + lane16).astype(F32) / F32(NY * N_GY - 1)
    dim = jnp.where(facing == 0, jnp.exp(-fraction), jnp.exp(-(1.0 - fraction)))
    picks_from = lax.broadcasted_iota(jnp.int32, (NY, NY), 0)
    picks_to = lax.broadcasted_iota(jnp.int32, (NY, NY), 1)
    picks = (picks_from == 4 * picks_to) | (
        (picks_from == 16 * (picks_to - 32)) & (picks_to >= 32)
    )
    picks = picks.astype(F32).astype(BF16)

    landed(max2, mr_sem.at[1])
    left(max2, ms_sem.at[1])
    for k in range(N_PLANE - 1):
        top = jnp.maximum(top, max2[k])
    speed = jnp.max(top, axis=1, keepdims=True)
    half_step = jnp.broadcast_to(0.5 * (0.8 / speed), (8, NY))

    def lit(z, t):
        rows = slice(8 * t, 8 * t + 8)
        rho = S[0, 0, z, rows, :] - half_step * CH[0, z, rows, :]
        NEW[0, 0, z, rows, :] = rho
        snap = rho.astype(BF16).astype(F32)
        SN[z, rows, :] = snap
        return snap * dim[rows]

    def folded(z, bit, t):
        span = 8 << bit
        if bit == 3:
            a, b = lit(z, t), lit(z + 8, t)
        else:
            a, b = folded(z, bit + 1, t), folded(z + (1 << bit), bit + 1, t)
        a = jnp.maximum(a, pltpu.roll(a, NY - span, 1))
        b = jnp.maximum(b, pltpu.roll(b, span, 1))
        return jnp.where(lane & span == 0, a, b)

    halves = []
    for t in range(2):
        a = folded(0, 0, t)
        for span in (4, 2, 1):
            a = jnp.maximum(a, pltpu.roll(a, NY - span, 1))
        halves.append(a)
    VT[...] = jnp.transpose(jnp.concatenate(halves + [jnp.zeros((NY - NX, NY), F32)], axis=0))

    @pl.when(g < SLABS)
    def _():
        for k in range(N_GY):
            to = lax.rem(gy + k, N_GY)
            part = {"grp": SLABS, "gx": lax.axis_index("gx"), "gy": to}
            remote(
                VT.at[pl.ds(8 * to, 1)], recv_v.at[g * N_GY + gy], vs_sem, vr_sem, part
            ).start()

    tiles = []
    whole = None
    for zg in range(4):
        for t in range(2):
            rows = slice(8 * t, 8 * t + 8)
            m = SN[4 * zg, rows, :]
            for j in range(1, 4):
                m = jnp.maximum(m, SN[4 * zg + j, rows, :])
            for span in (1, 2):
                m = jnp.maximum(m, pltpu.roll(m, NY - span, 1))
            for span in (1, 2):
                m = jnp.maximum(m, pltpu.roll(m, 8 - span, 0))
            tiles.append(m)
            whole = m if whole is None else jnp.maximum(whole, m)
    for span in (4, 8):
        whole = jnp.maximum(whole, pltpu.roll(whole, NY - span, 1))
    whole = jnp.maximum(whole, pltpu.roll(whole, 4, 0))
    left_hand = jnp.concatenate(tiles + [whole, whole], axis=0).astype(BF16)
    LH[...] = jnp.dot(left_hand, picks, preferred_element_type=F32)
    rows = jnp.concatenate([LH[pl.ds(0, 8, stride=4), :], LH[pl.ds(32, 8, stride=4), :]], axis=0)
    last = jnp.broadcast_to(LH[64:65, :], (NX, NY))
    SO[...] = jnp.where(lane16 < 32, rows, last).astype(BF16)

    @pl.when(g < SLABS)
    def _():
        part = {"grp": SLABS, "gx": lax.axis_index("gx"), "gy": gy}
        remote(SO, recv_o.at[g], os_sem, or_sem, part).start()

    def update(z, _):
        for i in range(1, NF):
            for t in range(2):
                rows = slice(8 * t, 8 * t + 8)
                NEW[0, i, z, rows, :] = S[0, i, z, rows, :] - half_step * CH[i, z, rows, :]
        return 0

    lax.fori_loop(0, NZ, update, 0)

    view_ref[...] = jnp.zeros(view_ref.shape, F32)
    fine_ref[...] = jnp.zeros(fine_ref.shape, BF16)
    coarse_ref[...] = jnp.zeros(coarse_ref.shape, BF16)

    @pl.when(g < SLABS)
    def _():
        out = pltpu.make_async_copy(NEW, new_ref, out_sem)
        out.start()
        rows16 = recv_v.at[pl.ds(0, N_GY)]
        left(rows16, vs_sem)
        left(SO, os_sem)
        out.wait()

    @pl.when(is_viz)
    def _():
        out = pltpu.make_async_copy(S, new_ref, out_sem)
        out.start()
        landed(recv_o, or_sem)
        for s in range(SLABS):
            block = recv_o[s]
            for zg in range(4):
                fine_ref[0, 4 * s + zg] = block[4 * zg : 4 * zg + 4, :32]
            coarse_ref[0, s] = block[0:1, 32:40]
        landed(recv_v, vr_sem)
        rows = []
        for s in range(SLABS):
            a = recv_v[s * N_GY]
            for k in range(1, N_GY):
                a = jnp.maximum(a, recv_v[s * N_GY + k])
            rows.append(a)
        view = jnp.concatenate(rows, axis=0)
        for x in range(NX):
            view_ref[0, x] = view[:, x : x + 1]
        out.wait()


def body(state, view_dir):
    any_space = pl.BlockSpec(memory_space=pl.ANY)
    vmem = pl.BlockSpec(memory_space=pltpu.VMEM)
    dma = pltpu.SemaphoreType.DMA
    return pl.pallas_call(
        kernel,
        out_shape=(
            jax.ShapeDtypeStruct(state.shape, F32),
            jax.ShapeDtypeStruct((1, NX, SLABS, 1), F32),
            jax.ShapeDtypeStruct((1, 12, 4, 32), BF16),
            jax.ShapeDtypeStruct((1, 3, 1, 8), BF16),
        ),
        in_specs=[any_space, pl.BlockSpec(memory_space=pltpu.SMEM)],
        out_specs=(any_space, vmem, vmem, vmem),
        scratch_shapes=[
            pltpu.VMEM(state.shape, F32),
            pltpu.VMEM((NF * WZ, WX, NY), F32),
            pltpu.VMEM((NF, NZ, NX, NY), F32),
            pltpu.VMEM((NF * NZ, 24, NY), F32),
            pltpu.VMEM((NZ + 1, NF, NX, NY), F32),
            pltpu.VMEM(state.shape, F32),
            pltpu.VMEM((NZ, NX, NY), F32),
            pltpu.VMEM((NF, NX, NY), F32),
            pltpu.VMEM((NF, NX, NY), F32),
            pltpu.VMEM((NY, NY), F32),
            pltpu.VMEM((80, NY), F32),
            pltpu.VMEM((NX, NY), BF16),
            pltpu.VMEM((2, NF, 2, NX, NY), BF16),
            pltpu.VMEM((2, NF, 2, NZ, NY), BF16),
            pltpu.VMEM((NF, NX, NY), BF16),
            pltpu.VMEM((2, NF, 2, NX, NY), BF16),
            pltpu.VMEM((2, NF, 2, NZ, NY), BF16),
            pltpu.VMEM((2, NF, NX, NY), BF16),
            pltpu.VMEM((1, 1, NY), F32),
            pltpu.VMEM((N_Z - 1, 1, NY), F32),
            pltpu.VMEM((1, 1, NY), F32),
            pltpu.VMEM((N_PLANE - 1, 1, NY), F32),
            pltpu.VMEM((SLABS * N_GY, 1, NY), F32),
            pltpu.VMEM((SLABS, NX, NY), BF16),
            dma, dma, dma((6,)), dma((6,)), dma((3,)), dma((3,)), dma, dma, dma, dma,
        ],
        compiler_params=pltpu.CompilerParams(collective_id=0, has_side_effects=True),
    )(state, view_dir)


def solution(mesh):
    in_specs = (P("grp", None, None, "gx", "gy"), P("gx"))
    out_specs = (
        P("grp", None, None, "gx", "gy"),
        P("grp", "gx", None, "gy"),
        P("grp", None, "gx", "gy"),
        P("grp", None, "gx", "gy"),
    )
    return jax.shard_map(body, mesh=mesh, in_specs=in_specs, out_specs=out_specs, check_vma=False)
```

```python
import jax
import jax.numpy as jnp
from jax import lax
from jax.experimental import pallas as pl
from jax.experimental.pallas import tpu as pltpu
from jax.sharding import PartitionSpec as P

F32 = jnp.float32
BF16 = jnp.bfloat16
MESH = pl.DeviceIdType.MESH

NF = 5
NZ = 16
NX = 16
NY = 128
N_GRP, N_GX, N_GY = 4, 4, 16
SLABS = 3
N_NEAR = 16
CHUNKS = 4
WZ = NZ + 4
WX = 32


def near_devices():
    g, x, y = lax.axis_index("grp"), lax.axis_index("gx"), lax.axis_index("gy")
    grps = [lax.rem(g + k, N_GRP) for k in range(N_GRP)]
    gxs = [lax.rem(x + k, N_GX) for k in range(N_GX)]
    other_core = y + 1 - 2 * lax.rem(y, 2)
    cores = [y, other_core, lax.rem(y + 8, N_GY), lax.rem(other_core + 8, N_GY)]
    in_plane = lax.rem(y, 8)
    ys = [y - in_plane + lax.rem(in_plane + 2 * k, 8) for k in range(4)]
    column = [{"grp": a, "gx": x, "gy": b} for a in grps for b in cores]
    plane = [{"grp": g, "gx": a, "gy": b} for a in gxs for b in ys]
    return column[1:], plane[1:]


def shifted(axis, step):
    place = {a: lax.axis_index(a) for a in ("grp", "gx", "gy")}
    count = {"grp": N_GRP, "gx": N_GX, "gy": N_GY}[axis]
    place[axis] = lax.rem(place[axis] + step + count, count)
    return place


def side(state, d):
    rho, p = state[0], state[4]
    v = state[1:4]
    m = [rho * a for a in v]
    energy = 2.5 * p + 0.5 * (m[0] * v[0] + m[1] * v[1] + m[2] * v[2])
    vd = state[d]
    fields = [rho, *m, energy]
    flux = [m[d - 1], m[0] * vd, m[1] * vd, m[2] * vd, (energy + p) * vd]
    flux[d] = flux[d] + p
    return fields, flux, jnp.abs(vd) + jnp.sqrt(1.4 * p / rho)


def face(q0, q1, q2, q3, d):
    low, up = [], []
    for a0, a1, a2, a3 in zip(q0, q1, q2, q3):
        a, b, c = a1 - a0, a2 - a1, a3 - a2
        left = jnp.maximum(jnp.minimum(a, b), jnp.minimum(jnp.maximum(a, b), 0.0))
        right = jnp.maximum(jnp.minimum(b, c), jnp.minimum(jnp.maximum(b, c), 0.0))
        low.append(a1 + 0.5 * left)
        up.append(a2 - 0.5 * right)
    ul, fl, rl = side(low, d)
    uu, fu, ru = side(up, d)
    wave = jnp.maximum(rl, ru)
    return [(a + b) - wave * (e - c) for a, b, c, e in zip(fl, fu, ul, uu)]


def kernel(
    state_ref, dir_ref, NEW, view_ref, fine_ref, coarse_ref,
    S, W, CH, FX, FZ, SN, PK, GY, VT, LH, SO,
    send_z, send_x, send_y, recv_z, recv_x, recv_y,
    max0, max1, max1v, max2, recv_v, recv_o,
    in_sem, out_sem, hs_sem, hr_sem, ms_sem, mr_sem, vs_sem, vr_sem, os_sem, or_sem,
):
    g, gy = lax.axis_index("grp"), lax.axis_index("gy")
    is_viz = g == SLABS
    depth = NZ // CHUNKS
    loads = []
    for n in range(CHUNKS):
        planes = pl.ds(n * depth, depth)
        loads.append(
            pltpu.make_async_copy(state_ref.at[:, :, planes], S.at[:, :, planes], in_sem.at[n])
        )
        loads[-1].start()

    @pl.when(is_viz)
    def _():
        pltpu.make_async_copy(state_ref, NEW, out_sem).start()

    z_parts, p_parts = near_devices()
    y_up, y_down = shifted("gy", 1), shifted("gy", -1)
    barrier = pltpu.get_barrier_semaphore()
    greeted = z_parts + p_parts + [y_up, y_down]
    for part in greeted:
        pl.semaphore_signal(barrier, inc=1, device_id=part, device_id_type=MESH)

    lane = lax.broadcasted_iota(jnp.int32, (8, NY), 1)
    row16 = lax.broadcasted_iota(jnp.int32, (NX, NY), 0)
    lane16 = lax.broadcasted_iota(jnp.int32, (NX, NY), 1)
    W2 = W.reshape(NF * WZ * WX, NY)


    def prims(z, carry):
        top, packed = carry[0], list(carry[1:])
        here = lax.shift_right_logical(lane, 2) == z
        for t in range(2):
            rows = slice(8 * t, 8 * t + 8)
            f = [S[0, i, z, rows, :] for i in range(NF)]
            inv = 1.0 / f[0]
            v = [a * inv for a in f[1:4]]
            p = 0.4 * (f[4] - 0.5 * (f[1] * v[0] + f[2] * v[1] + f[3] * v[2]))
            top = jnp.maximum(
                top,
                jnp.abs(v[0]) + jnp.abs(v[1]) + jnp.abs(v[2]) + 3.0 * jnp.sqrt(1.4 * p * inv),
            )
            for i, q in enumerate([f[0], *v, p]):
                W[i * WZ + 2 + z, 8 + 8 * t : 16 + 8 * t, :] = q
                packed[2 * i + t] = jnp.where(here, pltpu.roll(q, 4 * z + 2, 1), packed[2 * i + t])
        return (top, *packed)

    zero = jnp.zeros((8, NY), F32)
    carry = (zero,) * 11
    for n in range(CHUNKS):
        loads[n].wait()
        carry = lax.fori_loop(n * depth, (n + 1) * depth, prims, carry)
    max0[0] = jnp.max(carry[0], axis=0, keepdims=True)
    pl.semaphore_wait(barrier, len(greeted))

    def remote(src, dst, ssem, rsem, part):
        return pltpu.make_async_remote_copy(
            src_ref=src, dst_ref=dst, send_sem=ssem, recv_sem=rsem, device_id=part, device_id_type=MESH
        )

    for k, part in enumerate(z_parts):
        remote(max0.at[0], max1.at[k], ms_sem.at[0], mr_sem.at[0], part).start()
    for i in range(NF):
        PK[i] = jnp.concatenate([carry[1 + 2 * i], carry[2 + 2 * i]], axis=0)
        send_y[i] = PK[i].astype(BF16)
        for r in range(2):
            send_z[0, i, r] = W[i * WZ + NZ + r, 8:24, :].astype(BF16)
            send_z[1, i, r] = W[i * WZ + 2 + r, 8:24, :].astype(BF16)
            for way, row in ((0, 22 + r), (1, 8 + r)):
                halves = [
                    W2[pl.ds((i * WZ + 2 + 8 * h) * WX + row, 8, stride=WX), :] for h in range(2)
                ]
                send_x[way, i, r] = jnp.concatenate(halves, axis=0).astype(BF16)

    halo = []
    for way in range(2):
        step = 1 - 2 * way
        halo.append(
            remote(send_y, recv_y.at[way], hs_sem.at[way], hr_sem.at[way], (y_up, y_down)[way])
        )
    for way in range(2):
        step = 1 - 2 * way
        halo.append(
            remote(
                send_x.at[way], recv_x.at[way], hs_sem.at[2 + way], hr_sem.at[2 + way], shifted("gx", step)
            )
        )
    for way in range(2):
        step = 1 - 2 * way
        halo.append(
            remote(
                send_z.at[way], recv_z.at[way], hs_sem.at[4 + way], hr_sem.at[4 + way], shifted("grp", step)
            )
        )
    for copy in halo:
        copy.start()

    def z_face(p, _):
        for t in range(2):
            rows = slice(8 + 8 * t, 16 + 8 * t)
            q = [[W[i * WZ + p + j, rows, :] for i in range(NF)] for j in range(4)]
            for i, a in enumerate(face(*q, 1)):
                FZ[p, i, 8 * t : 8 * t + 8, :] = a
        return 0

    lax.fori_loop(2, NZ - 1, z_face, 0)

    halo[2].wait()
    halo[3].wait()
    for way, row in ((0, 6), (1, 24)):
        for i in range(NF):
            for r in range(2):
                rows = recv_x[way, i, r].astype(F32)
                for h in range(2):
                    W2[pl.ds((i * WZ + 2 + 8 * h) * WX + row + r, 8, stride=WX), :] = rows[8 * h : 8 * h + 8]
    FX2 = FX.reshape(NF * NZ * 24, NY)
    for h in range(2):
        q = [
            [W2[pl.ds((i * WZ + 2 + 8 * h) * WX + 22 + j, 8, stride=WX), :] for i in range(NF)]
            for j in range(4)
        ]
        for i, a in enumerate(face(*q, 2)):
            FX2[pl.ds((i * NZ + 8 * h) * 24 + 16, 8, stride=24), :] = a

    def x_pass(z, _):
        for t in range(2):
            q = [
                [W[i * WZ + 2 + z, 6 + j + 8 * t : 14 + j + 8 * t, :] for i in range(NF)] for j in range(4)
            ]
            for i, a in enumerate(face(*q, 2)):
                FX[i * NZ + z, 8 * t : 8 * t + 8, :] = a
        for t in range(2):
            rows = slice(8 * t, 8 * t + 8)
            for i in range(NF):
                CH[i, z, rows, :] = (
                    FX[i * NZ + z, 8 * t + 1 : 8 * t + 9, :] - FX[i * NZ + z, rows, :]
                )
        return 0

    lax.fori_loop(0, NZ, x_pass, 0)

    def landed(dst, sem):
        remote(dst, dst, ms_sem.at[2], sem, y_up).wait_recv()

    def left(src, sem):
        remote(src, src, sem, mr_sem.at[2], y_up).wait_send()

    landed(max1, mr_sem.at[0])
    left(max1, ms_sem.at[0])
    top = max0[0]
    for k in range(N_NEAR - 1):
        top = jnp.maximum(top, max1[k])
    max1v[0] = top
    for k, part in enumerate(p_parts):
        remote(max1v.at[0], max2.at[k], ms_sem.at[1], mr_sem.at[1], part).start()

    halo[0].wait()
    halo[1].wait()
    for t in range(2):
        rows = slice(8 * t, 8 * t + 8)
        q = [[], [], [], []]
        for i in range(NF):
            mine = PK[i, rows, :]
            other = recv_y[1, i, :, :].astype(F32)[rows]
            q[0].append(mine)
            q[1].append(pltpu.roll(mine, NY - 1, 1))
            q[2].append(pltpu.roll(other, NY - 2, 1))
            q[3].append(pltpu.roll(other, NY - 3, 1))
        for i, a in enumerate(face(*q, 3)):
            GY[i, rows, :] = a

    def y_pass(z, _):
        for t in range(2):
            rows = slice(8 * t, 8 * t + 8)
            q = [[], [], [], []]
            for i in range(NF):
                own = W[i * WZ + 2 + z, 8 + 8 * t : 16 + 8 * t, :]
                low = pltpu.roll(recv_y[0, i, :, :].astype(F32)[rows], lax.rem(NY - 4 * z, NY), 1)
                high = pltpu.roll(recv_y[1, i, :, :].astype(F32)[rows], 125 - 4 * z, 1)
                q[0].append(jnp.where(lane < 2, low, pltpu.roll(own, 2, 1)))
                q[1].append(jnp.where(lane < 1, pltpu.roll(low, NY - 1, 1), pltpu.roll(own, 1, 1)))
                q[2].append(own)
                q[3].append(jnp.where(lane == NY - 1, high, pltpu.roll(own, NY - 1, 1)))
            for i, a in enumerate(face(*q, 3)):
                end = pltpu.roll(GY[i, rows, :], 127 - 4 * z, 1)
                above = jnp.where(lane == NY - 1, end, pltpu.roll(a, NY - 1, 1))
                CH[i, z, rows, :] = CH[i, z, rows, :] + (above - a)
        return 0

    lax.fori_loop(0, NZ, y_pass, 0)

    halo[4].wait()
    halo[5].wait()
    for i in range(NF):
        for r in range(2):
            W[i * WZ + r, 8:24, :] = recv_z[0, i, r].astype(F32)
            W[i * WZ + 2 + NZ + r, 8:24, :] = recv_z[1, i, r].astype(F32)
    lax.fori_loop(0, 2, z_face, 0)
    lax.fori_loop(NZ - 1, NZ + 1, z_face, 0)

    def gather_change(z, _):
        for i in range(NF):
            CH[i, z] = CH[i, z] + (FZ[z + 1, i] - FZ[z, i])
        return 0

    lax.fori_loop(0, NZ, gather_change, 0)

    facing = jnp.zeros((NX, NY), jnp.int32)
    for x in range(NX):
        facing = jnp.where(row16 == x, dir_ref[x], facing)
    fraction = (gy * NY + lane16).astype(F32) / F32(NY * N_GY - 1)
    dim = jnp.where(facing == 0, jnp.exp(-fraction), jnp.exp(-(1.0 - fraction)))
    picks_from = lax.broadcasted_iota(jnp.int32, (NY, NY), 0)
    picks_to = lax.broadcasted_iota(jnp.int32, (NY, NY), 1)
    picks = (picks_from == 4 * picks_to) | (
        (picks_from == 16 * (picks_to - 32)) & (picks_to >= 32)
    )
    picks = picks.astype(F32).astype(BF16)

    landed(max2, mr_sem.at[1])
    left(max2, ms_sem.at[1])
    for k in range(N_NEAR - 1):
        top = jnp.maximum(top, max2[k])
    speed = jnp.max(top, axis=1, keepdims=True)
    half_step = jnp.broadcast_to(0.5 * (0.8 / speed), (8, NY))

    def lit(z, t):
        rows = slice(8 * t, 8 * t + 8)
        rho = S[0, 0, z, rows, :] - half_step * CH[0, z, rows, :]
        snap = rho.astype(BF16).astype(F32)
        SN[z, rows, :] = snap
        return snap * dim[rows]

    def folded(z, bit, t):
        span = 8 << bit
        if bit == 3:
            a, b = lit(z, t), lit(z + 8, t)
        else:
            a, b = folded(z, bit + 1, t), folded(z + (1 << bit), bit + 1, t)
        a = jnp.maximum(a, pltpu.roll(a, NY - span, 1))
        b = jnp.maximum(b, pltpu.roll(b, span, 1))
        return jnp.where(lane & span == 0, a, b)

    halves = []
    for t in range(2):
        a = folded(0, 0, t)
        for span in (4, 2, 1):
            a = jnp.maximum(a, pltpu.roll(a, NY - span, 1))
        halves.append(a)
    VT[...] = jnp.transpose(jnp.concatenate(halves + [jnp.zeros((NY - NX, NY), F32)], axis=0))

    @pl.when(g < SLABS)
    def _():
        for k in range(N_GY):
            to = lax.rem(gy + k, N_GY)
            part = {"grp": SLABS, "gx": lax.axis_index("gx"), "gy": to}
            remote(
                VT.at[pl.ds(8 * to, 1)], recv_v.at[g * N_GY + gy], vs_sem, vr_sem, part
            ).start()

    tiles = []
    whole = None
    for zg in range(4):
        for t in range(2):
            rows = slice(8 * t, 8 * t + 8)
            m = SN[4 * zg, rows, :]
            for j in range(1, 4):
                m = jnp.maximum(m, SN[4 * zg + j, rows, :])
            for span in (1, 2):
                m = jnp.maximum(m, pltpu.roll(m, NY - span, 1))
            for span in (1, 2):
                m = jnp.maximum(m, pltpu.roll(m, 8 - span, 0))
            tiles.append(m)
            whole = m if whole is None else jnp.maximum(whole, m)
    for span in (4, 8):
        whole = jnp.maximum(whole, pltpu.roll(whole, NY - span, 1))
    whole = jnp.maximum(whole, pltpu.roll(whole, 4, 0))
    left_hand = jnp.concatenate(tiles + [whole, whole], axis=0).astype(BF16)
    LH[...] = jnp.dot(left_hand, picks, preferred_element_type=F32)
    rows = jnp.concatenate([LH[pl.ds(0, 8, stride=4), :], LH[pl.ds(32, 8, stride=4), :]], axis=0)
    last = jnp.broadcast_to(LH[64:65, :], (NX, NY))
    SO[...] = jnp.where(lane16 < 32, rows, last).astype(BF16)

    @pl.when(g < SLABS)
    def _():
        part = {"grp": SLABS, "gx": lax.axis_index("gx"), "gy": gy}
        remote(SO, recv_o.at[g], os_sem, or_sem, part).start()

    def update(z, _):
        for i in range(NF):
            for t in range(2):
                rows = slice(8 * t, 8 * t + 8)
                NEW[0, i, z, rows, :] = S[0, i, z, rows, :] - half_step * CH[i, z, rows, :]
        return 0

    view_ref[...] = jnp.zeros(view_ref.shape, F32)
    fine_ref[...] = jnp.zeros(fine_ref.shape, BF16)
    coarse_ref[...] = jnp.zeros(coarse_ref.shape, BF16)

    @pl.when(g < SLABS)
    def _():
        lax.fori_loop(0, NZ, update, 0)
        rows16 = recv_v.at[pl.ds(0, N_GY)]
        left(rows16, vs_sem)
        left(SO, os_sem)

    @pl.when(is_viz)
    def _():
        landed(recv_o, or_sem)
        for s in range(SLABS):
            block = recv_o[s]
            for zg in range(4):
                fine_ref[0, 4 * s + zg] = block[4 * zg : 4 * zg + 4, :32]
            coarse_ref[0, 0, s : s + 1, :] = block[0:1, 32:40]
        landed(recv_v, vr_sem)
        for s in range(SLABS):
            a = recv_v[s * N_GY]
            for k in range(1, N_GY):
                a = jnp.maximum(a, recv_v[s * N_GY + k])
            view_ref[0, s] = a[:, :NX]
        pltpu.make_async_copy(state_ref, NEW, out_sem).wait()


def put_out(new_in, view_in, fine_in, coarse_in, new_out, view_out, fine_out, coarse_out, sems):
    copies = [
        pltpu.make_async_copy(a, b, sems.at[n])
        for n, (a, b) in enumerate(
            ((new_in, new_out), (view_in, view_out), (fine_in, fine_out), (coarse_in, coarse_out))
        )
    ]
    for copy in copies:
        copy.start()
    for copy in copies:
        copy.wait()


def body(state, view_dir):
    any_space = pl.BlockSpec(memory_space=pl.ANY)
    vmem = pl.BlockSpec(memory_space=pltpu.VMEM)
    dma = pltpu.SemaphoreType.DMA
    shapes = ((state.shape, F32), ((1, SLABS, 1, NX), F32), ((1, 12, 4, 32), BF16), ((1, 1, 3, 8), BF16))
    new_state, view, fine, coarse = pl.pallas_call(
        kernel,
        out_shape=tuple(pltpu.VMEM(*s) for s in shapes),
        in_specs=[any_space, pl.BlockSpec(memory_space=pltpu.SMEM)],
        out_specs=(vmem,) * 4,
        scratch_shapes=[
            pltpu.VMEM(state.shape, F32),
            pltpu.VMEM((NF * WZ, WX, NY), F32),
            pltpu.VMEM((NF, NZ, NX, NY), F32),
            pltpu.VMEM((NF * NZ, 24, NY), F32),
            pltpu.VMEM((NZ + 1, NF, NX, NY), F32),
                pltpu.VMEM((NZ, NX, NY), F32),
            pltpu.VMEM((NF, NX, NY), F32),
            pltpu.VMEM((NF, NX, NY), F32),
            pltpu.VMEM((NY, NY), F32),
            pltpu.VMEM((80, NY), F32),
            pltpu.VMEM((NX, NY), BF16),
            pltpu.VMEM((2, NF, 2, NX, NY), BF16),
            pltpu.VMEM((2, NF, 2, NZ, NY), BF16),
            pltpu.VMEM((NF, NX, NY), BF16),
            pltpu.VMEM((2, NF, 2, NX, NY), BF16),
            pltpu.VMEM((2, NF, 2, NZ, NY), BF16),
            pltpu.VMEM((2, NF, NX, NY), BF16),
            pltpu.VMEM((1, 1, NY), F32),
            pltpu.VMEM((N_NEAR - 1, 1, NY), F32),
            pltpu.VMEM((1, 1, NY), F32),
            pltpu.VMEM((N_NEAR - 1, 1, NY), F32),
            pltpu.VMEM((SLABS * N_GY, 1, NY), F32),
            pltpu.VMEM((SLABS, NX, NY), BF16),
            dma((CHUNKS,)), dma, dma((6,)), dma((6,)), dma((3,)), dma((3,)), dma, dma, dma, dma,
        ],
        compiler_params=pltpu.CompilerParams(collective_id=0, has_side_effects=True),
    )(state, view_dir)
    new_state, view, fine, coarse = pl.pallas_call(
        put_out,
        out_shape=tuple(jax.ShapeDtypeStruct(*s) for s in shapes),
        in_specs=[vmem] * 4,
        out_specs=(any_space,) * 4,
        scratch_shapes=[dma((4,))],
    )(*(pltpu.with_memory_space_constraint(a, pltpu.VMEM) for a in (new_state, view, fine, coarse)))
    return new_state, jnp.transpose(view, (0, 3, 1, 2)), fine, jnp.transpose(coarse, (0, 2, 1, 3))


def solution(mesh):
    in_specs = (P("grp", None, None, "gx", "gy"), P("gx"))
    out_specs = (
        P("grp", None, None, "gx", "gy"),
        P("grp", "gx", None, "gy"),
        P("grp", None, "gx", "gy"),
        P("grp", None, "gx", "gy"),
    )
    return jax.shard_map(body, mesh=mesh, in_specs=in_specs, out_specs=out_specs, check_vma=False)
```

```python
import jax
import jax.numpy as jnp
from jax import lax
from jax.experimental import pallas as pl
from jax.experimental.pallas import tpu as pltpu
from jax.sharding import PartitionSpec as P

F32 = jnp.float32
BF16 = jnp.bfloat16
MESH = pl.DeviceIdType.MESH

NF = 5
NZ = 16
NX = 16
NY = 128
N_GRP, N_GX, N_GY = 4, 4, 16
SLABS = 3
N_NEAR = 16
CHUNKS = 4
WZ = NZ + 4
WX = 32


def near_devices():
    g, x, y = lax.axis_index("grp"), lax.axis_index("gx"), lax.axis_index("gy")
    grps = [lax.rem(g + k, N_GRP) for k in range(N_GRP)]
    gxs = [lax.rem(x + k, N_GX) for k in range(N_GX)]
    other_core = y + 1 - 2 * lax.rem(y, 2)
    cores = [y, other_core, lax.rem(y + 8, N_GY), lax.rem(other_core + 8, N_GY)]
    in_plane = lax.rem(y, 8)
    ys = [y - in_plane + lax.rem(in_plane + 2 * k, 8) for k in range(4)]
    far_first = (2, 1, 3, 0)
    column = [{"grp": grps[k], "gx": x, "gy": b} for k in far_first for b in reversed(cores)]
    plane = [{"grp": g, "gx": gxs[k], "gy": ys[j]} for k in far_first for j in far_first]
    return column[:-1], plane[:-1]


def shifted(axis, step):
    place = {a: lax.axis_index(a) for a in ("grp", "gx", "gy")}
    count = {"grp": N_GRP, "gx": N_GX, "gy": N_GY}[axis]
    place[axis] = lax.rem(place[axis] + step + count, count)
    return place


def side(state, d):
    rho, p = state[0], state[4]
    v = state[1:4]
    m = [rho * a for a in v]
    energy = 2.5 * p + 0.5 * (m[0] * v[0] + m[1] * v[1] + m[2] * v[2])
    vd = state[d]
    fields = [rho, *m, energy]
    flux = [m[d - 1], m[0] * vd, m[1] * vd, m[2] * vd, (energy + p) * vd]
    flux[d] = flux[d] + p
    return fields, flux, jnp.abs(vd) + jnp.sqrt(1.4 * p / rho)


def face(q0, q1, q2, q3, d):
    low, up = [], []
    for a0, a1, a2, a3 in zip(q0, q1, q2, q3):
        a, b, c = a1 - a0, a2 - a1, a3 - a2
        left = jnp.maximum(jnp.minimum(a, b), jnp.minimum(jnp.maximum(a, b), 0.0))
        right = jnp.maximum(jnp.minimum(b, c), jnp.minimum(jnp.maximum(b, c), 0.0))
        low.append(a1 + 0.5 * left)
        up.append(a2 - 0.5 * right)
    ul, fl, rl = side(low, d)
    uu, fu, ru = side(up, d)
    wave = jnp.maximum(rl, ru)
    return [(a + b) - wave * (e - c) for a, b, c, e in zip(fl, fu, ul, uu)]


def kernel(
    state_ref, dir_ref, NEW, view_ref, fine_ref, coarse_ref,
    S, W, CH, FX, FZ, QY, SN, PK, GY, VT, LH, SO,
    send_z, send_x, send_y, recv_z, recv_x, recv_y,
    max0, max1, max1v, max2, recv_v, recv_o,
    in_sem, out_sem, hs_sem, hr_sem, ms_sem, mr_sem, vs_sem, vr_sem, os_sem, or_sem,
):
    g, gy = lax.axis_index("grp"), lax.axis_index("gy")
    is_viz = g == SLABS
    depth = NZ // CHUNKS
    loads = []
    for n in range(CHUNKS):
        planes = pl.ds(n * depth, depth)
        loads.append(
            pltpu.make_async_copy(state_ref.at[:, :, planes], S.at[:, :, planes], in_sem.at[n])
        )
        loads[-1].start()

    @pl.when(is_viz)
    def _():
        pltpu.make_async_copy(state_ref, NEW, out_sem).start()

    z_parts, p_parts = near_devices()
    y_up, y_down = shifted("gy", 1), shifted("gy", -1)
    barrier = pltpu.get_barrier_semaphore()
    greeted = z_parts[:8] + p_parts[:8] + [y_up, y_down] + z_parts[8:] + p_parts[8:]
    for part in greeted:
        pl.semaphore_signal(barrier, inc=1, device_id=part, device_id_type=MESH)

    lane = lax.broadcasted_iota(jnp.int32, (8, NY), 1)
    row16 = lax.broadcasted_iota(jnp.int32, (NX, NY), 0)
    lane16 = lax.broadcasted_iota(jnp.int32, (NX, NY), 1)
    W2 = W.reshape(NF * WZ * WX, NY)


    def prims(z, carry):
        top, packed = carry[0], list(carry[1:])
        here = lax.shift_right_logical(lane, 3) == z
        for t in range(2):
            rows = slice(8 * t, 8 * t + 8)
            f = [S[0, i, z, rows, :] for i in range(NF)]
            inv = 1.0 / f[0]
            v = [a * inv for a in f[1:4]]
            p = 0.4 * (f[4] - 0.5 * (f[1] * v[0] + f[2] * v[1] + f[3] * v[2]))
            top = jnp.maximum(
                top,
                jnp.abs(v[0]) + jnp.abs(v[1]) + jnp.abs(v[2]) + 3.0 * jnp.sqrt(1.4 * p * inv),
            )
            for i, q in enumerate([f[0], *v, p]):
                W[i * WZ + 2 + z, 8 + 8 * t : 16 + 8 * t, :] = q
                packed[2 * i + t] = jnp.where(
                    here, pltpu.roll(q, lax.rem(8 * z + 4, NY), 1), packed[2 * i + t]
                )
                for j, turn in enumerate((2, 1, NY - 1)):
                    QY[j, i * NZ + z, rows, :] = pltpu.roll(q, turn, 1)
        return (top, *packed)

    zero = jnp.zeros((8, NY), F32)
    carry = (zero,) * 11
    for n in range(CHUNKS):
        loads[n].wait()
        carry = lax.fori_loop(n * depth, (n + 1) * depth, prims, carry)
    max0[0] = jnp.max(carry[0], axis=0, keepdims=True)
    pl.semaphore_wait(barrier, len(greeted))

    def remote(src, dst, ssem, rsem, part):
        return pltpu.make_async_remote_copy(
            src_ref=src, dst_ref=dst, send_sem=ssem, recv_sem=rsem, device_id=part, device_id_type=MESH
        )

    for k, part in enumerate(z_parts):
        remote(max0.at[0], max1.at[k], ms_sem.at[0], mr_sem.at[0], part).start()
    for i in range(NF):
        PK[i] = jnp.concatenate([carry[1 + 2 * i], carry[2 + 2 * i]], axis=0)
        send_y[i] = PK[i].astype(BF16)
        for r in range(2):
            send_z[0, i, r] = W[i * WZ + NZ + r, 8:24, :].astype(BF16)
            send_z[1, i, r] = W[i * WZ + 2 + r, 8:24, :].astype(BF16)
            for way, row in ((0, 22 + r), (1, 8 + r)):
                halves = [
                    W2[pl.ds((i * WZ + 2 + 8 * h) * WX + row, 8, stride=WX), :] for h in range(2)
                ]
                send_x[way, i, r] = jnp.concatenate(halves, axis=0).astype(BF16)

    halo = []
    for way in range(2):
        step = 1 - 2 * way
        halo.append(
            remote(send_y, recv_y.at[way], hs_sem.at[way], hr_sem.at[way], (y_up, y_down)[way])
        )
    for way in range(2):
        step = 1 - 2 * way
        halo.append(
            remote(
                send_x.at[way], recv_x.at[way], hs_sem.at[2 + way], hr_sem.at[2 + way], shifted("gx", step)
            )
        )
    for way in range(2):
        step = 1 - 2 * way
        halo.append(
            remote(
                send_z.at[way], recv_z.at[way], hs_sem.at[4 + way], hr_sem.at[4 + way], shifted("grp", step)
            )
        )
    for copy in halo:
        copy.start()

    def z_face(p, _):
        for t in range(2):
            rows = slice(8 + 8 * t, 16 + 8 * t)
            q = [[W[i * WZ + p + j, rows, :] for i in range(NF)] for j in range(4)]
            for i, a in enumerate(face(*q, 1)):
                FZ[p, i, 8 * t : 8 * t + 8, :] = a
        return 0

    lax.fori_loop(2, NZ - 1, z_face, 0)

    def y_face(z, _):
        for t in range(2):
            rows = slice(8 * t, 8 * t + 8)
            q = [[QY[j, i * NZ + z, rows, :] for i in range(NF)] for j in range(3)]
            own = [W[i * WZ + 2 + z, 8 + 8 * t : 16 + 8 * t, :] for i in range(NF)]
            for i, a in enumerate(face(q[0], q[1], own, q[2], 3)):
                CH[i, z, rows, :] = a
        return 0

    lax.fori_loop(0, NZ, y_face, 0)

    halo[0].wait()
    halo[1].wait()
    slot = lane & 7
    for t in range(2):
        rows = slice(8 * t, 8 * t + 8)
        q = [[], [], [], []]
        for i in range(NF):
            own = PK[i, rows, :]
            low = recv_y[0, i].astype(F32)[rows]
            high = recv_y[1, i].astype(F32)[rows]
            back = pltpu.roll(own, NY - 1, 1)
            q[0].append(
                jnp.where(
                    slot == 2, own, jnp.where(slot == 3, pltpu.roll(own, 2, 1), pltpu.roll(low, 2, 1))
                )
            )
            q[1].append(
                jnp.where(
                    slot == 2, back, jnp.where(slot == 4, pltpu.roll(low, 1, 1), pltpu.roll(own, 1, 1))
                )
            )
            q[2].append(jnp.where(slot == 2, pltpu.roll(high, NY - 2, 1), own))
            q[3].append(
                jnp.where(
                    slot == 2,
                    pltpu.roll(high, NY - 3, 1),
                    jnp.where(slot == 3, pltpu.roll(high, NY - 1, 1), back),
                )
            )
        for i, a in enumerate(face(*q, 3)):
            GY[i, rows, :] = a

    def landed(dst, sem):
        remote(dst, dst, ms_sem.at[2], sem, y_up).wait_recv()

    def left(src, sem):
        remote(src, src, sem, mr_sem.at[2], y_up).wait_send()

    landed(max1, mr_sem.at[0])
    left(max1, ms_sem.at[0])
    top = max0[0]
    for k in range(N_NEAR - 1):
        top = jnp.maximum(top, max1[k])
    max1v[0] = top
    for k, part in enumerate(p_parts):
        remote(max1v.at[0], max2.at[k], ms_sem.at[1], mr_sem.at[1], part).start()

    halo[2].wait()
    halo[3].wait()
    for way, row in ((0, 6), (1, 24)):
        for i in range(NF):
            for r in range(2):
                rows = recv_x[way, i, r].astype(F32)
                for h in range(2):
                    W2[pl.ds((i * WZ + 2 + 8 * h) * WX + row + r, 8, stride=WX), :] = rows[8 * h : 8 * h + 8]
    FX2 = FX.reshape(NF * NZ * 24, NY)
    for h in range(2):
        q = [
            [W2[pl.ds((i * WZ + 2 + 8 * h) * WX + 22 + j, 8, stride=WX), :] for i in range(NF)]
            for j in range(4)
        ]
        for i, a in enumerate(face(*q, 2)):
            FX2[pl.ds((i * NZ + 8 * h) * 24 + 16, 8, stride=24), :] = a

    def x_pass(z, _):
        for t in range(2):
            q = [
                [W[i * WZ + 2 + z, 6 + j + 8 * t : 14 + j + 8 * t, :] for i in range(NF)] for j in range(4)
            ]
            for i, a in enumerate(face(*q, 2)):
                FX[i * NZ + z, 8 * t : 8 * t + 8, :] = a
        for t in range(2):
            rows = slice(8 * t, 8 * t + 8)
            for i in range(NF):
                ends = pltpu.roll(GY[i, rows, :], lax.rem(2 * NY - 4 - 8 * z, NY), 1)
                a = jnp.where((lane < 2) | (lane == NY - 1), ends, CH[i, z, rows, :])
                above = jnp.where(lane == NY - 1, pltpu.roll(ends, 1, 1), pltpu.roll(a, NY - 1, 1))
                CH[i, z, rows, :] = (above - a) + (
                    FX[i * NZ + z, 8 * t + 1 : 8 * t + 9, :] - FX[i * NZ + z, rows, :]
                )
        return 0

    lax.fori_loop(0, NZ, x_pass, 0)

    halo[4].wait()
    halo[5].wait()
    for i in range(NF):
        for r in range(2):
            W[i * WZ + r, 8:24, :] = recv_z[0, i, r].astype(F32)
            W[i * WZ + 2 + NZ + r, 8:24, :] = recv_z[1, i, r].astype(F32)
    lax.fori_loop(0, 2, z_face, 0)
    lax.fori_loop(NZ - 1, NZ + 1, z_face, 0)

    def gather_change(z, _):
        for i in range(NF):
            CH[i, z] = CH[i, z] + (FZ[z + 1, i] - FZ[z, i])
        return 0

    lax.fori_loop(0, NZ, gather_change, 0)

    facing = jnp.zeros((NX, NY), jnp.int32)
    for x in range(NX):
        facing = jnp.where(row16 == x, dir_ref[x], facing)
    fraction = (gy * NY + lane16).astype(F32) / F32(NY * N_GY - 1)
    dim = jnp.where(facing == 0, jnp.exp(-fraction), jnp.exp(-(1.0 - fraction)))
    picks_from = lax.broadcasted_iota(jnp.int32, (NY, NY), 0)
    picks_to = lax.broadcasted_iota(jnp.int32, (NY, NY), 1)
    picks = (picks_from == 4 * picks_to) | (
        (picks_from == 16 * (picks_to - 32)) & (picks_to >= 32)
    )
    picks = picks.astype(F32).astype(BF16)

    landed(max2, mr_sem.at[1])
    left(max2, ms_sem.at[1])
    for k in range(N_NEAR - 1):
        top = jnp.maximum(top, max2[k])
    speed = jnp.max(top, axis=1, keepdims=True)
    half_step = jnp.broadcast_to(0.5 * (0.8 / speed), (8, NY))

    def lit(z, t):
        rows = slice(8 * t, 8 * t + 8)
        rho = S[0, 0, z, rows, :] - half_step * CH[0, z, rows, :]
        snap = rho.astype(BF16).astype(F32)
        SN[z, rows, :] = snap
        return snap * dim[rows]

    def folded(z, bit, t):
        span = 8 << bit
        if bit == 3:
            a, b = lit(z, t), lit(z + 8, t)
        else:
            a, b = folded(z, bit + 1, t), folded(z + (1 << bit), bit + 1, t)
        a = jnp.maximum(a, pltpu.roll(a, NY - span, 1))
        b = jnp.maximum(b, pltpu.roll(b, span, 1))
        return jnp.where(lane & span == 0, a, b)

    halves = []
    for t in range(2):
        a = folded(0, 0, t)
        for span in (4, 2, 1):
            a = jnp.maximum(a, pltpu.roll(a, NY - span, 1))
        halves.append(a)
    VT[...] = jnp.transpose(jnp.concatenate(halves + [jnp.zeros((NY - NX, NY), F32)], axis=0))

    @pl.when(g < SLABS)
    def _():
        for k in range(N_GY):
            to = lax.rem(gy + k, N_GY)
            part = {"grp": SLABS, "gx": lax.axis_index("gx"), "gy": to}
            remote(
                VT.at[pl.ds(8 * to, 1)], recv_v.at[g * N_GY + gy], vs_sem, vr_sem, part
            ).start()

    tiles = []
    whole = None
    for zg in range(4):
        for t in range(2):
            rows = slice(8 * t, 8 * t + 8)
            m = SN[4 * zg, rows, :]
            for j in range(1, 4):
                m = jnp.maximum(m, SN[4 * zg + j, rows, :])
            for span in (1, 2):
                m = jnp.maximum(m, pltpu.roll(m, NY - span, 1))
            for span in (1, 2):
                m = jnp.maximum(m, pltpu.roll(m, 8 - span, 0))
            tiles.append(m)
            whole = m if whole is None else jnp.maximum(whole, m)
    for span in (4, 8):
        whole = jnp.maximum(whole, pltpu.roll(whole, NY - span, 1))
    whole = jnp.maximum(whole, pltpu.roll(whole, 4, 0))
    left_hand = jnp.concatenate(tiles + [whole, whole], axis=0).astype(BF16)
    LH[...] = jnp.dot(left_hand, picks, preferred_element_type=F32)
    rows = jnp.concatenate([LH[pl.ds(0, 8, stride=4), :], LH[pl.ds(32, 8, stride=4), :]], axis=0)
    last = jnp.broadcast_to(LH[64:65, :], (NX, NY))
    SO[...] = jnp.where(lane16 < 32, rows, last).astype(BF16)

    @pl.when(g < SLABS)
    def _():
        part = {"grp": SLABS, "gx": lax.axis_index("gx"), "gy": gy}
        remote(SO, recv_o.at[g], os_sem, or_sem, part).start()

    def update(z, _):
        for i in range(NF):
            for t in range(2):
                rows = slice(8 * t, 8 * t + 8)
                NEW[0, i, z, rows, :] = S[0, i, z, rows, :] - half_step * CH[i, z, rows, :]
        return 0

    view_ref[...] = jnp.zeros(view_ref.shape, F32)
    fine_ref[...] = jnp.zeros(fine_ref.shape, BF16)
    coarse_ref[...] = jnp.zeros(coarse_ref.shape, BF16)

    @pl.when(g < SLABS)
    def _():
        lax.fori_loop(0, NZ, update, 0)
        rows16 = recv_v.at[pl.ds(0, N_GY)]
        left(rows16, vs_sem)
        left(SO, os_sem)

    @pl.when(is_viz)
    def _():
        landed(recv_o, or_sem)
        for s in range(SLABS):
            block = recv_o[s]
            for zg in range(4):
                fine_ref[0, 4 * s + zg] = block[4 * zg : 4 * zg + 4, :32]
            coarse_ref[0, 0, s : s + 1, :] = block[0:1, 32:40]
        landed(recv_v, vr_sem)
        for s in range(SLABS):
            a = recv_v[s * N_GY]
            for k in range(1, N_GY):
                a = jnp.maximum(a, recv_v[s * N_GY + k])
            view_ref[0, s] = a[:, :NX]
        pltpu.make_async_copy(state_ref, NEW, out_sem).wait()


def put_out(new_in, view_in, fine_in, coarse_in, new_out, view_out, fine_out, coarse_out, sems):
    copies = [
        pltpu.make_async_copy(a, b, sems.at[n])
        for n, (a, b) in enumerate(
            ((new_in, new_out), (view_in, view_out), (fine_in, fine_out), (coarse_in, coarse_out))
        )
    ]
    for copy in copies:
        copy.start()
    for copy in copies:
        copy.wait()


def body(state, view_dir):
    any_space = pl.BlockSpec(memory_space=pl.ANY)
    vmem = pl.BlockSpec(memory_space=pltpu.VMEM)
    dma = pltpu.SemaphoreType.DMA
    shapes = ((state.shape, F32), ((1, SLABS, 1, NX), F32), ((1, 12, 4, 32), BF16), ((1, 1, 3, 8), BF16))
    new_state, view, fine, coarse = pl.pallas_call(
        kernel,
        out_shape=tuple(pltpu.VMEM(*s) for s in shapes),
        in_specs=[any_space, pl.BlockSpec(memory_space=pltpu.SMEM)],
        out_specs=(vmem,) * 4,
        scratch_shapes=[
            pltpu.VMEM(state.shape, F32),
            pltpu.VMEM((NF * WZ, WX, NY), F32),
            pltpu.VMEM((NF, NZ, NX, NY), F32),
            pltpu.VMEM((NF * NZ, 24, NY), F32),
            pltpu.VMEM((NZ + 1, NF, NX, NY), F32),
                pltpu.VMEM((3, NF * NZ, NX, NY), F32),
        pltpu.VMEM((NZ, NX, NY), F32),
            pltpu.VMEM((NF, NX, NY), F32),
            pltpu.VMEM((NF, NX, NY), F32),
            pltpu.VMEM((NY, NY), F32),
            pltpu.VMEM((80, NY), F32),
            pltpu.VMEM((NX, NY), BF16),
            pltpu.VMEM((2, NF, 2, NX, NY), BF16),
            pltpu.VMEM((2, NF, 2, NZ, NY), BF16),
            pltpu.VMEM((NF, NX, NY), BF16),
            pltpu.VMEM((2, NF, 2, NX, NY), BF16),
            pltpu.VMEM((2, NF, 2, NZ, NY), BF16),
            pltpu.VMEM((2, NF, NX, NY), BF16),
            pltpu.VMEM((1, 1, NY), F32),
            pltpu.VMEM((N_NEAR - 1, 1, NY), F32),
            pltpu.VMEM((1, 1, NY), F32),
            pltpu.VMEM((N_NEAR - 1, 1, NY), F32),
            pltpu.VMEM((SLABS * N_GY, 1, NY), F32),
            pltpu.VMEM((SLABS, NX, NY), BF16),
            dma((CHUNKS,)), dma, dma((6,)), dma((6,)), dma((3,)), dma((3,)), dma, dma, dma, dma,
        ],
        compiler_params=pltpu.CompilerParams(collective_id=0, has_side_effects=True),
    )(state, view_dir)
    new_state, view, fine, coarse = pl.pallas_call(
        put_out,
        out_shape=tuple(jax.ShapeDtypeStruct(*s) for s in shapes),
        in_specs=[vmem] * 4,
        out_specs=(any_space,) * 4,
        scratch_shapes=[dma((4,))],
    )(*(pltpu.with_memory_space_constraint(a, pltpu.VMEM) for a in (new_state, view, fine, coarse)))
    return new_state, jnp.transpose(view, (0, 3, 1, 2)), fine, jnp.transpose(coarse, (0, 2, 1, 3))


def solution(mesh):
    in_specs = (P("grp", None, None, "gx", "gy"), P("gx"))
    out_specs = (
        P("grp", None, None, "gx", "gy"),
        P("grp", "gx", None, "gy"),
        P("grp", None, "gx", "gy"),
        P("grp", None, "gx", "gy"),
    )
    return jax.shard_map(body, mesh=mesh, in_specs=in_specs, out_specs=out_specs, check_vma=False)
```

```python
import jax
import jax.numpy as jnp
from jax import lax
from jax.experimental import pallas as pl
from jax.experimental.pallas import tpu as pltpu
from jax.sharding import PartitionSpec as P

F32 = jnp.float32
BF16 = jnp.bfloat16
MESH = pl.DeviceIdType.MESH

NF = 5
NZ = 16
NX = 16
NY = 128
N_GRP, N_GX, N_GY = 4, 4, 16
SLABS = 3
N_NEAR = 16
CHUNKS = 4
WZ = NZ + 4
WX = 32


def near_devices():
    g, x, y = lax.axis_index("grp"), lax.axis_index("gx"), lax.axis_index("gy")
    grps = [lax.rem(g + k, N_GRP) for k in range(N_GRP)]
    gxs = [lax.rem(x + k, N_GX) for k in range(N_GX)]
    other_core = y + 1 - 2 * lax.rem(y, 2)
    cores = [y, other_core, lax.rem(y + 8, N_GY), lax.rem(other_core + 8, N_GY)]
    in_plane = lax.rem(y, 8)
    ys = [y - in_plane + lax.rem(in_plane + 2 * k, 8) for k in range(4)]
    far_first = (2, 1, 3, 0)
    column = [{"grp": grps[k], "gx": x, "gy": b} for k in far_first for b in reversed(cores)]
    plane = [{"grp": g, "gx": gxs[k], "gy": ys[j]} for k in far_first for j in far_first]
    return column[:-1], plane[:-1]


def shifted(axis, step):
    place = {a: lax.axis_index(a) for a in ("grp", "gx", "gy")}
    count = {"grp": N_GRP, "gx": N_GX, "gy": N_GY}[axis]
    place[axis] = lax.rem(place[axis] + step + count, count)
    return place


def side(state, d):
    rho, p = state[0], state[4]
    v = state[1:4]
    m = [rho * a for a in v]
    energy = 2.5 * p + 0.5 * (m[0] * v[0] + m[1] * v[1] + m[2] * v[2])
    vd = state[d]
    fields = [rho, *m, energy]
    flux = [m[d - 1], m[0] * vd, m[1] * vd, m[2] * vd, (energy + p) * vd]
    flux[d] = flux[d] + p
    return fields, flux, jnp.abs(vd) + jnp.sqrt(1.4 * p / rho)


def face(q0, q1, q2, q3, d):
    low, up = [], []
    for a0, a1, a2, a3 in zip(q0, q1, q2, q3):
        a, b, c = a1 - a0, a2 - a1, a3 - a2
        left = jnp.maximum(jnp.minimum(a, b), jnp.minimum(jnp.maximum(a, b), 0.0))
        right = jnp.maximum(jnp.minimum(b, c), jnp.minimum(jnp.maximum(b, c), 0.0))
        low.append(a1 + 0.5 * left)
        up.append(a2 - 0.5 * right)
    ul, fl, rl = side(low, d)
    uu, fu, ru = side(up, d)
    wave = jnp.maximum(rl, ru)
    return [(a + b) - wave * (e - c) for a, b, c, e in zip(fl, fu, ul, uu)]


def kernel(
    state_ref, dir_ref, NEW, view_ref, fine_ref, coarse_ref,
    S, W, CH, FX, FZ, QY, ST, CT, DT, RV, PK, GY, LH, SO,
    send_z, send_x, send_y, recv_z, recv_x, recv_y,
    max0, max1, max1v, max2, recv_v, recv_o,
    in_sem, out_sem, hs_sem, hr_sem, ms_sem, mr_sem, vs_sem, vr_sem, os_sem, or_sem,
):
    g, gy = lax.axis_index("grp"), lax.axis_index("gy")
    is_viz = g == SLABS
    depth = NZ // CHUNKS
    loads = []
    for n in range(CHUNKS):
        planes = pl.ds(n * depth, depth)
        loads.append(
            pltpu.make_async_copy(state_ref.at[:, :, planes], S.at[:, :, planes], in_sem.at[n])
        )
        loads[-1].start()

    @pl.when(is_viz)
    def _():
        pltpu.make_async_copy(state_ref, NEW, out_sem).start()

    z_parts, p_parts = near_devices()
    y_up, y_down = shifted("gy", 1), shifted("gy", -1)
    barrier = pltpu.get_barrier_semaphore()
    greeted = z_parts[:8] + p_parts[:8] + [y_up, y_down] + z_parts[8:] + p_parts[8:]
    for part in greeted:
        pl.semaphore_signal(barrier, inc=1, device_id=part, device_id_type=MESH)

    lane = lax.broadcasted_iota(jnp.int32, (8, NY), 1)
    row16 = lax.broadcasted_iota(jnp.int32, (NX, NY), 0)
    lane16 = lax.broadcasted_iota(jnp.int32, (NX, NY), 1)
    W2 = W.reshape(NF * WZ * WX, NY)


    def prims(z, carry):
        top, packed = carry[0], list(carry[1:])
        here = lax.shift_right_logical(lane, 3) == z
        for t in range(2):
            rows = slice(8 * t, 8 * t + 8)
            f = [S[0, i, z, rows, :] for i in range(NF)]
            inv = 1.0 / f[0]
            v = [a * inv for a in f[1:4]]
            p = 0.4 * (f[4] - 0.5 * (f[1] * v[0] + f[2] * v[1] + f[3] * v[2]))
            top = jnp.maximum(
                top,
                jnp.abs(v[0]) + jnp.abs(v[1]) + jnp.abs(v[2]) + 3.0 * jnp.sqrt(1.4 * p * inv),
            )
            for i, q in enumerate([f[0], *v, p]):
                W[i * WZ + 2 + z, 8 + 8 * t : 16 + 8 * t, :] = q
                packed[2 * i + t] = jnp.where(
                    here, pltpu.roll(q, lax.rem(8 * z + 4, NY), 1), packed[2 * i + t]
                )
                for j, turn in enumerate((2, 1, NY - 1)):
                    QY[j, i * NZ + z, rows, :] = pltpu.roll(q, turn, 1)
        return (top, *packed)

    zero = jnp.zeros((8, NY), F32)
    carry = (zero,) * 11
    for n in range(CHUNKS):
        loads[n].wait()
        carry = lax.fori_loop(n * depth, (n + 1) * depth, prims, carry)
    top = jnp.max(jnp.max(carry[0], axis=0, keepdims=True), axis=1, keepdims=True)
    max0[0] = jnp.broadcast_to(top, (1, NY))
    pl.semaphore_wait(barrier, len(greeted))

    def remote(src, dst, ssem, rsem, part):
        return pltpu.make_async_remote_copy(
            src_ref=src, dst_ref=dst, send_sem=ssem, recv_sem=rsem, device_id=part, device_id_type=MESH
        )

    for k, part in enumerate(z_parts):
        remote(max0.at[0], max1.at[k], ms_sem.at[0], mr_sem.at[0], part).start()
    for i in range(NF):
        PK[i] = jnp.concatenate([carry[1 + 2 * i], carry[2 + 2 * i]], axis=0)
        send_y[i] = PK[i].astype(BF16)
        for r in range(2):
            send_z[0, i, r] = W[i * WZ + NZ + r, 8:24, :].astype(BF16)
            send_z[1, i, r] = W[i * WZ + 2 + r, 8:24, :].astype(BF16)
            for way, row in ((0, 22 + r), (1, 8 + r)):
                halves = [
                    W2[pl.ds((i * WZ + 2 + 8 * h) * WX + row, 8, stride=WX), :] for h in range(2)
                ]
                send_x[way, i, r] = jnp.concatenate(halves, axis=0).astype(BF16)

    halo = []
    for way in range(2):
        step = 1 - 2 * way
        halo.append(
            remote(send_y, recv_y.at[way], hs_sem.at[way], hr_sem.at[way], (y_up, y_down)[way])
        )
    for way in range(2):
        step = 1 - 2 * way
        halo.append(
            remote(
                send_x.at[way], recv_x.at[way], hs_sem.at[2 + way], hr_sem.at[2 + way], shifted("gx", step)
            )
        )
    for way in range(2):
        step = 1 - 2 * way
        halo.append(
            remote(
                send_z.at[way], recv_z.at[way], hs_sem.at[4 + way], hr_sem.at[4 + way], shifted("grp", step)
            )
        )
    for copy in halo:
        copy.start()

    def z_face(p, _):
        for t in range(2):
            rows = slice(8 + 8 * t, 16 + 8 * t)
            q = [[W[i * WZ + p + j, rows, :] for i in range(NF)] for j in range(4)]
            for i, a in enumerate(face(*q, 1)):
                FZ[p, i, 8 * t : 8 * t + 8, :] = a
        return 0

    lax.fori_loop(2, NZ - 1, z_face, 0)

    def y_face(z, _):
        for t in range(2):
            rows = slice(8 * t, 8 * t + 8)
            q = [[QY[j, i * NZ + z, rows, :] for i in range(NF)] for j in range(3)]
            own = [W[i * WZ + 2 + z, 8 + 8 * t : 16 + 8 * t, :] for i in range(NF)]
            for i, a in enumerate(face(q[0], q[1], own, q[2], 3)):
                CH[i, z, rows, :] = a
        return 0

    lax.fori_loop(0, NZ, y_face, 0)

    halo[0].wait()
    halo[1].wait()
    slot = lane & 7
    for t in range(2):
        rows = slice(8 * t, 8 * t + 8)
        q = [[], [], [], []]
        for i in range(NF):
            own = PK[i, rows, :]
            low = recv_y[0, i].astype(F32)[rows]
            high = recv_y[1, i].astype(F32)[rows]
            back = pltpu.roll(own, NY - 1, 1)
            q[0].append(
                jnp.where(
                    slot == 2, own, jnp.where(slot == 3, pltpu.roll(own, 2, 1), pltpu.roll(low, 2, 1))
                )
            )
            q[1].append(
                jnp.where(
                    slot == 2, back, jnp.where(slot == 4, pltpu.roll(low, 1, 1), pltpu.roll(own, 1, 1))
                )
            )
            q[2].append(jnp.where(slot == 2, pltpu.roll(high, NY - 2, 1), own))
            q[3].append(
                jnp.where(
                    slot == 2,
                    pltpu.roll(high, NY - 3, 1),
                    jnp.where(slot == 3, pltpu.roll(high, NY - 1, 1), back),
                )
            )
        for i, a in enumerate(face(*q, 3)):
            GY[i, rows, :] = a

    def landed(dst, sem):
        remote(dst, dst, ms_sem.at[2], sem, y_up).wait_recv()

    def left(src, sem):
        remote(src, src, sem, mr_sem.at[2], y_up).wait_send()

    landed(max1, mr_sem.at[0])
    left(max1, ms_sem.at[0])
    top = max0[0]
    for k in range(N_NEAR - 1):
        top = jnp.maximum(top, max1[k])
    max1v[0] = top
    for k, part in enumerate(p_parts):
        remote(max1v.at[0], max2.at[k], ms_sem.at[1], mr_sem.at[1], part).start()

    halo[2].wait()
    halo[3].wait()
    for way, row in ((0, 6), (1, 24)):
        for i in range(NF):
            for r in range(2):
                rows = recv_x[way, i, r].astype(F32)
                for h in range(2):
                    W2[pl.ds((i * WZ + 2 + 8 * h) * WX + row + r, 8, stride=WX), :] = rows[8 * h : 8 * h + 8]
    FX2 = FX.reshape(NF * NZ * 24, NY)
    for h in range(2):
        q = [
            [W2[pl.ds((i * WZ + 2 + 8 * h) * WX + 22 + j, 8, stride=WX), :] for i in range(NF)]
            for j in range(4)
        ]
        for i, a in enumerate(face(*q, 2)):
            FX2[pl.ds((i * NZ + 8 * h) * 24 + 16, 8, stride=24), :] = a

    def x_pass(z, _):
        for t in range(2):
            q = [
                [W[i * WZ + 2 + z, 6 + j + 8 * t : 14 + j + 8 * t, :] for i in range(NF)] for j in range(4)
            ]
            for i, a in enumerate(face(*q, 2)):
                FX[i * NZ + z, 8 * t : 8 * t + 8, :] = a
        for t in range(2):
            rows = slice(8 * t, 8 * t + 8)
            for i in range(NF):
                ends = pltpu.roll(GY[i, rows, :], lax.rem(2 * NY - 4 - 8 * z, NY), 1)
                a = jnp.where((lane < 2) | (lane == NY - 1), ends, CH[i, z, rows, :])
                above = jnp.where(lane == NY - 1, pltpu.roll(ends, 1, 1), pltpu.roll(a, NY - 1, 1))
                CH[i, z, rows, :] = (above - a) + (
                    FX[i * NZ + z, 8 * t + 1 : 8 * t + 9, :] - FX[i * NZ + z, rows, :]
                )
        return 0

    lax.fori_loop(0, NZ, x_pass, 0)

    halo[4].wait()
    halo[5].wait()
    for i in range(NF):
        for r in range(2):
            W[i * WZ + r, 8:24, :] = recv_z[0, i, r].astype(F32)
            W[i * WZ + 2 + NZ + r, 8:24, :] = recv_z[1, i, r].astype(F32)
    lax.fori_loop(0, 2, z_face, 0)
    lax.fori_loop(NZ - 1, NZ + 1, z_face, 0)

    def gather_change(z, _):
        for i in range(NF):
            CH[i, z] = CH[i, z] + (FZ[z + 1, i] - FZ[z, i])
        return 0

    lax.fori_loop(0, NZ, gather_change, 0)

    for h in range(2):
        planes = slice(8 * h, 8 * h + 8)
        ST[h] = jnp.transpose(S[0, 0, planes].reshape(NY, NY))
        CT[h] = jnp.transpose(CH[0, planes].reshape(NY, NY))
    cell_x = lane & (NX - 1)
    facing = jnp.zeros((8, NY), jnp.int32)
    for x in range(NX):
        facing = jnp.where(cell_x == x, dir_ref[x], facing)
    for n in range(NY // 8):
        y = lax.broadcasted_iota(jnp.int32, (8, NY), 0) + (gy * NY + 8 * n)
        fraction = y.astype(F32) / F32(NY * N_GY - 1)
        dim = jnp.where(facing == 0, jnp.exp(-fraction), jnp.exp(-(1.0 - fraction)))
        DT[8 * n : 8 * n + 8, :] = dim
    picks_from = lax.broadcasted_iota(jnp.int32, (NY, NY), 0)
    picks_to = lax.broadcasted_iota(jnp.int32, (NY, NY), 1)
    picks = (picks_from == 4 * picks_to) | (
        (picks_from == 16 * (picks_to - 32)) & (picks_to >= 32)
    )
    picks = picks.astype(F32).astype(BF16)

    landed(max2, mr_sem.at[1])
    left(max2, ms_sem.at[1])
    rows = [max1v[0]] + [max2[k] for k in range(N_NEAR - 1)]
    while len(rows) > 1:
        rows = [jnp.maximum(p, q) for p, q in zip(rows[::2], rows[1::2])]
    half_step = jnp.broadcast_to(0.5 * (0.8 / rows[0]), (8, NY))

    view_ref[...] = jnp.zeros(view_ref.shape, F32)
    fine_ref[...] = jnp.zeros(fine_ref.shape, BF16)
    coarse_ref[...] = jnp.zeros(coarse_ref.shape, BF16)

    @pl.when(g < SLABS)
    def _():
        for h in range(2):
            lit = []
            for n in range(NY // 8):
                rows = slice(8 * n, 8 * n + 8)
                rho = ST[h, rows, :] - half_step * CT[h, rows, :]
                lit.append(rho.astype(BF16).astype(F32) * DT[rows, :])
            while len(lit) > 1:
                lit = [jnp.maximum(p, q) for p, q in zip(lit[::2], lit[1::2])]
            RV[h] = jnp.max(lit[0], axis=0, keepdims=True)
        for k in range(N_GY):
            to = lax.rem(gy + k, N_GY)
            part = {"grp": SLABS, "gx": lax.axis_index("gx"), "gy": to}
            remote(RV.at[to // 8], recv_v.at[g * N_GY + gy], vs_sem, vr_sem, part).start()

        def update(i, z):
            for t in range(2):
                rows = slice(8 * t, 8 * t + 8)
                NEW[0, i, z, rows, :] = S[0, i, z, rows, :] - half_step * CH[i, z, rows, :]

        for z in range(NZ):
            update(0, z)
        tiles = []
        whole = None
        for zg in range(4):
            for t in range(2):
                rows = slice(8 * t, 8 * t + 8)
                m = NEW[0, 0, 4 * zg, rows, :]
                for j in range(1, 4):
                    m = jnp.maximum(m, NEW[0, 0, 4 * zg + j, rows, :])
                for span in (1, 2):
                    m = jnp.maximum(m, pltpu.roll(m, NY - span, 1))
                for span in (1, 2):
                    m = jnp.maximum(m, pltpu.roll(m, 8 - span, 0))
                tiles.append(m)
                whole = m if whole is None else jnp.maximum(whole, m)
        for span in (4, 8):
            whole = jnp.maximum(whole, pltpu.roll(whole, NY - span, 1))
        whole = jnp.maximum(whole, pltpu.roll(whole, 4, 0))
        left_hand = jnp.concatenate(tiles + [whole, whole], axis=0).astype(BF16)
        LH[...] = jnp.dot(left_hand, picks, preferred_element_type=F32)
        rows = jnp.concatenate([LH[pl.ds(0, 8, stride=4), :], LH[pl.ds(32, 8, stride=4), :]], axis=0)
        last = jnp.broadcast_to(LH[64:65, :], (NX, NY))
        SO[...] = jnp.where(lane16 < 32, rows, last).astype(BF16)

        part = {"grp": SLABS, "gx": lax.axis_index("gx"), "gy": gy}
        remote(SO, recv_o.at[g], os_sem, or_sem, part).start()

        def update_rest(z, _):
            for i in range(1, NF):
                update(i, z)
            return 0

        lax.fori_loop(0, NZ, update_rest, 0)
        left(recv_v.at[pl.ds(0, N_GY)], vs_sem)
        left(SO, os_sem)

    @pl.when(is_viz)
    def _():
        landed(recv_o, or_sem)
        for s in range(SLABS):
            block = recv_o[s]
            for zg in range(4):
                fine_ref[0, 4 * s + zg] = block[4 * zg : 4 * zg + 4, :32]
            coarse_ref[0, 0, s : s + 1, :] = block[0:1, 32:40]
        landed(recv_v, vr_sem)
        for s in range(SLABS):
            a = recv_v[s * N_GY]
            for k in range(1, N_GY):
                a = jnp.maximum(a, recv_v[s * N_GY + k])
            a = pltpu.roll(jnp.broadcast_to(a, (8, NY)), lax.rem(NY - NX * lax.rem(gy, 8), NY), 1)
            view_ref[0, s] = a[0:1, :NX]
        pltpu.make_async_copy(state_ref, NEW, out_sem).wait()


def put_out(new_in, view_in, fine_in, coarse_in, new_out, view_out, fine_out, coarse_out, sems):
    copies = [
        pltpu.make_async_copy(a, b, sems.at[n])
        for n, (a, b) in enumerate(
            ((new_in, new_out), (view_in, view_out), (fine_in, fine_out), (coarse_in, coarse_out))
        )
    ]
    for copy in copies:
        copy.start()
    for copy in copies:
        copy.wait()


def body(state, view_dir):
    any_space = pl.BlockSpec(memory_space=pl.ANY)
    vmem = pl.BlockSpec(memory_space=pltpu.VMEM)
    dma = pltpu.SemaphoreType.DMA
    shapes = ((state.shape, F32), ((1, SLABS, 1, NX), F32), ((1, 12, 4, 32), BF16), ((1, 1, 3, 8), BF16))
    new_state, view, fine, coarse = pl.pallas_call(
        kernel,
        out_shape=tuple(pltpu.VMEM(*s) for s in shapes),
        in_specs=[any_space, pl.BlockSpec(memory_space=pltpu.SMEM)],
        out_specs=(vmem,) * 4,
        scratch_shapes=[
            pltpu.VMEM(state.shape, F32),
            pltpu.VMEM((NF * WZ, WX, NY), F32),
            pltpu.VMEM((NF, NZ, NX, NY), F32),
            pltpu.VMEM((NF * NZ, 24, NY), F32),
            pltpu.VMEM((NZ + 1, NF, NX, NY), F32),
                pltpu.VMEM((3, NF * NZ, NX, NY), F32),
            pltpu.VMEM((2, NY, NY), F32),
            pltpu.VMEM((2, NY, NY), F32),
            pltpu.VMEM((NY, NY), F32),
            pltpu.VMEM((2, 1, NY), F32),
            pltpu.VMEM((NF, NX, NY), F32),
            pltpu.VMEM((NF, NX, NY), F32),
            pltpu.VMEM((80, NY), F32),
            pltpu.VMEM((NX, NY), BF16),
            pltpu.VMEM((2, NF, 2, NX, NY), BF16),
            pltpu.VMEM((2, NF, 2, NZ, NY), BF16),
            pltpu.VMEM((NF, NX, NY), BF16),
            pltpu.VMEM((2, NF, 2, NX, NY), BF16),
            pltpu.VMEM((2, NF, 2, NZ, NY), BF16),
            pltpu.VMEM((2, NF, NX, NY), BF16),
            pltpu.VMEM((1, 1, NY), F32),
            pltpu.VMEM((N_NEAR - 1, 1, NY), F32),
            pltpu.VMEM((1, 1, NY), F32),
            pltpu.VMEM((N_NEAR - 1, 1, NY), F32),
            pltpu.VMEM((SLABS * N_GY, 1, NY), F32),
            pltpu.VMEM((SLABS, NX, NY), BF16),
            dma((CHUNKS,)), dma, dma((6,)), dma((6,)), dma((3,)), dma((3,)), dma, dma, dma, dma,
        ],
        compiler_params=pltpu.CompilerParams(collective_id=0, has_side_effects=True),
    )(state, view_dir)
    new_state, view, fine, coarse = pl.pallas_call(
        put_out,
        out_shape=tuple(jax.ShapeDtypeStruct(*s) for s in shapes),
        in_specs=[vmem] * 4,
        out_specs=(any_space,) * 4,
        scratch_shapes=[dma((4,))],
    )(*(pltpu.with_memory_space_constraint(a, pltpu.VMEM) for a in (new_state, view, fine, coarse)))
    return new_state, jnp.transpose(view, (0, 3, 1, 2)), fine, jnp.transpose(coarse, (0, 2, 1, 3))


def solution(mesh):
    in_specs = (P("grp", None, None, "gx", "gy"), P("gx"))
    out_specs = (
        P("grp", None, None, "gx", "gy"),
        P("grp", "gx", None, "gy"),
        P("grp", None, "gx", "gy"),
        P("grp", None, "gx", "gy"),
    )
    return jax.shard_map(body, mesh=mesh, in_specs=in_specs, out_specs=out_specs, check_vma=False)
```

```python
import jax
import jax.numpy as jnp
from jax import lax
from jax.experimental import pallas as pl
from jax.experimental.pallas import tpu as pltpu
from jax.sharding import PartitionSpec as P

F32 = jnp.float32
BF16 = jnp.bfloat16
MESH = pl.DeviceIdType.MESH

NF = 5
NZ = 16
NX = 16
NY = 128
N_GRP, N_GX, N_GY = 4, 4, 16
SLABS = 3
N_NEAR = 16
CHUNKS = 4
WZ = NZ + 4
WX = 32


def near_devices():
    g, x, y = lax.axis_index("grp"), lax.axis_index("gx"), lax.axis_index("gy")
    grps = [lax.rem(g + k, N_GRP) for k in range(N_GRP)]
    gxs = [lax.rem(x + k, N_GX) for k in range(N_GX)]
    other_core = y + 1 - 2 * lax.rem(y, 2)
    cores = [y, other_core, lax.rem(y + 8, N_GY), lax.rem(other_core + 8, N_GY)]
    in_plane = lax.rem(y, 8)
    ys = [y - in_plane + lax.rem(in_plane + 2 * k, 8) for k in range(4)]
    far_first = (2, 1, 3, 0)
    column = [{"grp": grps[k], "gx": x, "gy": b} for k in far_first for b in reversed(cores)]
    plane = [{"grp": g, "gx": gxs[k], "gy": ys[j]} for k in far_first for j in far_first]
    return column[:-1], plane[:-1]


def shifted(axis, step):
    place = {a: lax.axis_index(a) for a in ("grp", "gx", "gy")}
    count = {"grp": N_GRP, "gx": N_GX, "gy": N_GY}[axis]
    place[axis] = lax.rem(place[axis] + step + count, count)
    return place


def side(state, d):
    rho, p = state[0], state[4]
    v = state[1:4]
    m = [rho * a for a in v]
    energy = 2.5 * p + 0.5 * (m[0] * v[0] + m[1] * v[1] + m[2] * v[2])
    vd = state[d]
    fields = [rho, *m, energy]
    flux = [m[d - 1], m[0] * vd, m[1] * vd, m[2] * vd, (energy + p) * vd]
    flux[d] = flux[d] + p
    return fields, flux, jnp.abs(vd) + jnp.sqrt(1.4 * p / rho)


def face(q0, q1, q2, q3, d):
    low, up = [], []
    for a0, a1, a2, a3 in zip(q0, q1, q2, q3):
        a, b, c = a1 - a0, a2 - a1, a3 - a2
        left = jnp.maximum(jnp.minimum(a, b), jnp.minimum(jnp.maximum(a, b), 0.0))
        right = jnp.maximum(jnp.minimum(b, c), jnp.minimum(jnp.maximum(b, c), 0.0))
        low.append(a1 + 0.5 * left)
        up.append(a2 - 0.5 * right)
    ul, fl, rl = side(low, d)
    uu, fu, ru = side(up, d)
    wave = jnp.maximum(rl, ru)
    return [(a + b) - wave * (e - c) for a, b, c, e in zip(fl, fu, ul, uu)]


def kernel(
    state_ref, dir_ref, NEW, view_ref, fine_ref, coarse_ref,
    S, W, CH, FX, FZ, QY, ST, CT, DT, RV, PK, GY, LH, SO,
    send_z, send_x, send_y, recv_z, recv_x, recv_y,
    max0, max1, max1v, max2, recv_v, recv_o,
    in_sem, out_sem, hs_sem, hr_sem, ms_sem, mr_sem, vs_sem, vr_sem, os_sem, or_sem,
):
    g, gy = lax.axis_index("grp"), lax.axis_index("gy")
    is_viz = g == SLABS
    depth = NZ // CHUNKS
    loads = []
    for n in range(CHUNKS):
        planes = pl.ds(n * depth, depth)
        loads.append(
            pltpu.make_async_copy(state_ref.at[:, :, planes], S.at[:, :, planes], in_sem.at[n])
        )
        loads[-1].start()

    @pl.when(is_viz)
    def _():
        pltpu.make_async_copy(state_ref, NEW, out_sem).start()

    z_parts, p_parts = near_devices()
    y_up, y_down = shifted("gy", 1), shifted("gy", -1)
    barrier = pltpu.get_barrier_semaphore()
    greeted = z_parts[:8] + p_parts[:8] + [y_up, y_down] + z_parts[8:] + p_parts[8:]
    for part in greeted:
        pl.semaphore_signal(barrier, inc=1, device_id=part, device_id_type=MESH)

    lane = lax.broadcasted_iota(jnp.int32, (8, NY), 1)
    row16 = lax.broadcasted_iota(jnp.int32, (NX, NY), 0)
    lane16 = lax.broadcasted_iota(jnp.int32, (NX, NY), 1)
    W2 = W.reshape(NF * WZ * WX, NY)


    def prims(z, carry):
        top, packed = carry[0], list(carry[1:])
        here = lax.shift_right_logical(lane, 3) == z
        for t in range(2):
            rows = slice(8 * t, 8 * t + 8)
            f = [S[0, i, z, rows, :] for i in range(NF)]
            inv = 1.0 / f[0]
            v = [a * inv for a in f[1:4]]
            p = 0.4 * (f[4] - 0.5 * (f[1] * v[0] + f[2] * v[1] + f[3] * v[2]))
            top = jnp.maximum(
                top,
                jnp.abs(v[0]) + jnp.abs(v[1]) + jnp.abs(v[2]) + 3.0 * jnp.sqrt(1.4 * p * inv),
            )
            for i, q in enumerate([f[0], *v, p]):
                W[i * WZ + 2 + z, 8 + 8 * t : 16 + 8 * t, :] = q
                packed[2 * i + t] = jnp.where(
                    here, pltpu.roll(q, lax.rem(8 * z + 4, NY), 1), packed[2 * i + t]
                )
        return (top, *packed)

    zero = jnp.zeros((8, NY), F32)
    carry = (zero,) * 11
    for n in range(CHUNKS):
        loads[n].wait()
        carry = lax.fori_loop(n * depth, (n + 1) * depth, prims, carry)
    top = jnp.max(jnp.max(carry[0], axis=0, keepdims=True), axis=1, keepdims=True)
    max0[0] = jnp.broadcast_to(top, (1, NY))
    pl.semaphore_wait(barrier, len(greeted))

    def remote(src, dst, ssem, rsem, part):
        return pltpu.make_async_remote_copy(
            src_ref=src, dst_ref=dst, send_sem=ssem, recv_sem=rsem, device_id=part, device_id_type=MESH
        )

    for k, part in enumerate(z_parts):
        remote(max0.at[0], max1.at[k], ms_sem.at[0], mr_sem.at[0], part).start()
    for i in range(NF):
        PK[i] = jnp.concatenate([carry[1 + 2 * i], carry[2 + 2 * i]], axis=0)
        send_y[i] = PK[i].astype(BF16)
        for r in range(2):
            send_z[0, i, r] = W[i * WZ + NZ + r, 8:24, :].astype(BF16)
            send_z[1, i, r] = W[i * WZ + 2 + r, 8:24, :].astype(BF16)
            for way, row in ((0, 22 + r), (1, 8 + r)):
                halves = [
                    W2[pl.ds((i * WZ + 2 + 8 * h) * WX + row, 8, stride=WX), :] for h in range(2)
                ]
                send_x[way, i, r] = jnp.concatenate(halves, axis=0).astype(BF16)

    halo = []
    for way in range(2):
        step = 1 - 2 * way
        halo.append(
            remote(send_y, recv_y.at[way], hs_sem.at[way], hr_sem.at[way], (y_up, y_down)[way])
        )
    for way in range(2):
        step = 1 - 2 * way
        halo.append(
            remote(
                send_x.at[way], recv_x.at[way], hs_sem.at[2 + way], hr_sem.at[2 + way], shifted("gx", step)
            )
        )
    for way in range(2):
        step = 1 - 2 * way
        halo.append(
            remote(
                send_z.at[way], recv_z.at[way], hs_sem.at[4 + way], hr_sem.at[4 + way], shifted("grp", step)
            )
        )
    for copy in halo:
        copy.start()

    def y_shifts(z, _):
        for i in range(NF):
            for t in range(2):
                rows = slice(8 * t, 8 * t + 8)
                q = W[i * WZ + 2 + z, 8 + 8 * t : 16 + 8 * t, :]
                for j, turn in enumerate((2, 1, NY - 1)):
                    QY[j, i * NZ + z, rows, :] = pltpu.roll(q, turn, 1)
        return 0

    lax.fori_loop(0, NZ, y_shifts, 0)

    def z_face(p, _):
        for t in range(2):
            rows = slice(8 + 8 * t, 16 + 8 * t)
            q = [[W[i * WZ + p + j, rows, :] for i in range(NF)] for j in range(4)]
            for i, a in enumerate(face(*q, 1)):
                FZ[p, i, 8 * t : 8 * t + 8, :] = a
        return 0

    lax.fori_loop(2, NZ - 1, z_face, 0)

    def y_face(z, _):
        for t in range(2):
            rows = slice(8 * t, 8 * t + 8)
            q = [[QY[j, i * NZ + z, rows, :] for i in range(NF)] for j in range(3)]
            own = [W[i * WZ + 2 + z, 8 + 8 * t : 16 + 8 * t, :] for i in range(NF)]
            for i, a in enumerate(face(q[0], q[1], own, q[2], 3)):
                CH[i, z, rows, :] = a
        return 0

    lax.fori_loop(0, NZ, y_face, 0)

    halo[0].wait()
    halo[1].wait()
    slot = lane & 7
    for t in range(2):
        rows = slice(8 * t, 8 * t + 8)
        q = [[], [], [], []]
        for i in range(NF):
            own = PK[i, rows, :]
            low = recv_y[0, i].astype(F32)[rows]
            high = recv_y[1, i].astype(F32)[rows]
            back = pltpu.roll(own, NY - 1, 1)
            q[0].append(
                jnp.where(
                    slot == 2, own, jnp.where(slot == 3, pltpu.roll(own, 2, 1), pltpu.roll(low, 2, 1))
                )
            )
            q[1].append(
                jnp.where(
                    slot == 2, back, jnp.where(slot == 4, pltpu.roll(low, 1, 1), pltpu.roll(own, 1, 1))
                )
            )
            q[2].append(jnp.where(slot == 2, pltpu.roll(high, NY - 2, 1), own))
            q[3].append(
                jnp.where(
                    slot == 2,
                    pltpu.roll(high, NY - 3, 1),
                    jnp.where(slot == 3, pltpu.roll(high, NY - 1, 1), back),
                )
            )
        for i, a in enumerate(face(*q, 3)):
            GY[i, rows, :] = a

    def landed(dst, sem):
        remote(dst, dst, ms_sem.at[2], sem, y_up).wait_recv()

    def left(src, sem):
        remote(src, src, sem, mr_sem.at[2], y_up).wait_send()

    landed(max1, mr_sem.at[0])
    left(max1, ms_sem.at[0])
    top = max0[0]
    for k in range(N_NEAR - 1):
        top = jnp.maximum(top, max1[k])
    max1v[0] = top
    for k, part in enumerate(p_parts):
        remote(max1v.at[0], max2.at[k], ms_sem.at[1], mr_sem.at[1], part).start()

    halo[2].wait()
    halo[3].wait()
    for way, row in ((0, 6), (1, 24)):
        for i in range(NF):
            for r in range(2):
                rows = recv_x[way, i, r].astype(F32)
                for h in range(2):
                    W2[pl.ds((i * WZ + 2 + 8 * h) * WX + row + r, 8, stride=WX), :] = rows[8 * h : 8 * h + 8]
    FX2 = FX.reshape(NF * NZ * 24, NY)
    for h in range(2):
        q = [
            [W2[pl.ds((i * WZ + 2 + 8 * h) * WX + 22 + j, 8, stride=WX), :] for i in range(NF)]
            for j in range(4)
        ]
        for i, a in enumerate(face(*q, 2)):
            FX2[pl.ds((i * NZ + 8 * h) * 24 + 16, 8, stride=24), :] = a

    def x_pass(z, _):
        for t in range(2):
            q = [
                [W[i * WZ + 2 + z, 6 + j + 8 * t : 14 + j + 8 * t, :] for i in range(NF)] for j in range(4)
            ]
            for i, a in enumerate(face(*q, 2)):
                FX[i * NZ + z, 8 * t : 8 * t + 8, :] = a
        for t in range(2):
            rows = slice(8 * t, 8 * t + 8)
            for i in range(NF):
                ends = pltpu.roll(GY[i, rows, :], lax.rem(2 * NY - 4 - 8 * z, NY), 1)
                a = jnp.where((lane < 2) | (lane == NY - 1), ends, CH[i, z, rows, :])
                above = jnp.where(lane == NY - 1, pltpu.roll(ends, 1, 1), pltpu.roll(a, NY - 1, 1))
                CH[i, z, rows, :] = (above - a) + (
                    FX[i * NZ + z, 8 * t + 1 : 8 * t + 9, :] - FX[i * NZ + z, rows, :]
                )
        return 0

    lax.fori_loop(0, NZ, x_pass, 0)

    halo[4].wait()
    halo[5].wait()
    for i in range(NF):
        for r in range(2):
            W[i * WZ + r, 8:24, :] = recv_z[0, i, r].astype(F32)
            W[i * WZ + 2 + NZ + r, 8:24, :] = recv_z[1, i, r].astype(F32)
    lax.fori_loop(0, 2, z_face, 0)
    lax.fori_loop(NZ - 1, NZ + 1, z_face, 0)

    def gather_change(z, _):
        for i in range(NF):
            CH[i, z] = CH[i, z] + (FZ[z + 1, i] - FZ[z, i])
        return 0

    lax.fori_loop(0, NZ, gather_change, 0)

    for h in range(2):
        planes = slice(8 * h, 8 * h + 8)
        ST[h] = jnp.transpose(S[0, 0, planes].reshape(NY, NY))
        CT[h] = jnp.transpose(CH[0, planes].reshape(NY, NY))
    cell_x = lane & (NX - 1)
    facing = jnp.zeros((8, NY), jnp.int32)
    for x in range(NX):
        facing = jnp.where(cell_x == x, dir_ref[x], facing)
    for n in range(NY // 8):
        y = lax.broadcasted_iota(jnp.int32, (8, NY), 0) + (gy * NY + 8 * n)
        fraction = y.astype(F32) / F32(NY * N_GY - 1)
        dim = jnp.where(facing == 0, jnp.exp(-fraction), jnp.exp(-(1.0 - fraction)))
        DT[8 * n : 8 * n + 8, :] = dim
    picks_from = lax.broadcasted_iota(jnp.int32, (NY, NY), 0)
    picks_to = lax.broadcasted_iota(jnp.int32, (NY, NY), 1)
    picks = (picks_from == 4 * picks_to) | (
        (picks_from == 16 * (picks_to - 32)) & (picks_to >= 32)
    )
    picks = picks.astype(F32).astype(BF16)

    landed(max2, mr_sem.at[1])
    left(max2, ms_sem.at[1])
    rows = [max1v[0]] + [max2[k] for k in range(N_NEAR - 1)]
    while len(rows) > 1:
        rows = [jnp.maximum(p, q) for p, q in zip(rows[::2], rows[1::2])]
    half_step = jnp.broadcast_to(0.5 * (0.8 / rows[0]), (8, NY))

    view_ref[...] = jnp.zeros(view_ref.shape, F32)
    fine_ref[...] = jnp.zeros(fine_ref.shape, BF16)
    coarse_ref[...] = jnp.zeros(coarse_ref.shape, BF16)

    @pl.when(g < SLABS)
    def _():
        for h in range(2):
            lit = []
            for n in range(NY // 8):
                rows = slice(8 * n, 8 * n + 8)
                rho = ST[h, rows, :] - half_step * CT[h, rows, :]
                lit.append(rho.astype(BF16).astype(F32) * DT[rows, :])
            while len(lit) > 1:
                lit = [jnp.maximum(p, q) for p, q in zip(lit[::2], lit[1::2])]
            RV[h] = jnp.max(lit[0], axis=0, keepdims=True)
        half, pair = gy // 8, lax.rem(gy, 8) // 2
        for z_half in (1 - half, half):
            for k in (2, 1, 3, 0):
                for core in range(2):
                    to = 8 * z_half + 2 * lax.rem(pair + k, 4) + core
                    part = {"grp": SLABS, "gx": lax.axis_index("gx"), "gy": to}
                    remote(RV.at[z_half], recv_v.at[g * N_GY + gy], vs_sem, vr_sem, part).start()

        def update(i, z):
            for t in range(2):
                rows = slice(8 * t, 8 * t + 8)
                NEW[0, i, z, rows, :] = S[0, i, z, rows, :] - half_step * CH[i, z, rows, :]

        for z in range(NZ):
            update(0, z)
        tiles = []
        whole = None
        for zg in range(4):
            for t in range(2):
                rows = slice(8 * t, 8 * t + 8)
                m = NEW[0, 0, 4 * zg, rows, :]
                for j in range(1, 4):
                    m = jnp.maximum(m, NEW[0, 0, 4 * zg + j, rows, :])
                for span in (1, 2):
                    m = jnp.maximum(m, pltpu.roll(m, NY - span, 1))
                for span in (1, 2):
                    m = jnp.maximum(m, pltpu.roll(m, 8 - span, 0))
                tiles.append(m)
                whole = m if whole is None else jnp.maximum(whole, m)
        for span in (4, 8):
            whole = jnp.maximum(whole, pltpu.roll(whole, NY - span, 1))
        whole = jnp.maximum(whole, pltpu.roll(whole, 4, 0))
        left_hand = jnp.concatenate(tiles + [whole, whole], axis=0).astype(BF16)
        LH[...] = jnp.dot(left_hand, picks, preferred_element_type=F32)
        rows = jnp.concatenate([LH[pl.ds(0, 8, stride=4), :], LH[pl.ds(32, 8, stride=4), :]], axis=0)
        last = jnp.broadcast_to(LH[64:65, :], (NX, NY))
        SO[...] = jnp.where(lane16 < 32, rows, last).astype(BF16)

        part = {"grp": SLABS, "gx": lax.axis_index("gx"), "gy": gy}
        remote(SO, recv_o.at[g], os_sem, or_sem, part).start()

        def update_rest(z, _):
            for i in range(1, NF):
                update(i, z)
            return 0

        lax.fori_loop(0, NZ, update_rest, 0)
        left(recv_v.at[pl.ds(0, N_GY)], vs_sem)
        left(SO, os_sem)

    @pl.when(is_viz)
    def _():
        landed(recv_o, or_sem)
        for s in range(SLABS):
            block = recv_o[s]
            for zg in range(4):
                fine_ref[0, 4 * s + zg] = block[4 * zg : 4 * zg + 4, :32]
            coarse_ref[0, 0, s : s + 1, :] = block[0:1, 32:40]
        landed(recv_v, vr_sem)
        for s in range(SLABS):
            rows = [recv_v[s * N_GY + k] for k in range(N_GY)]
            while len(rows) > 1:
                rows = [jnp.maximum(p, q) for p, q in zip(rows[::2], rows[1::2])]
            a = rows[0]
            a = pltpu.roll(jnp.broadcast_to(a, (8, NY)), lax.rem(NY - NX * lax.rem(gy, 8), NY), 1)
            view_ref[0, s] = a[0:1, :NX]
        pltpu.make_async_copy(state_ref, NEW, out_sem).wait()


def put_out(new_in, view_in, fine_in, coarse_in, new_out, view_out, fine_out, coarse_out, sems):
    copies = [
        pltpu.make_async_copy(a, b, sems.at[n])
        for n, (a, b) in enumerate(
            ((new_in, new_out), (view_in, view_out), (fine_in, fine_out), (coarse_in, coarse_out))
        )
    ]
    for copy in copies:
        copy.start()
    for copy in copies:
        copy.wait()


def body(state, view_dir):
    any_space = pl.BlockSpec(memory_space=pl.ANY)
    vmem = pl.BlockSpec(memory_space=pltpu.VMEM)
    dma = pltpu.SemaphoreType.DMA
    shapes = ((state.shape, F32), ((1, SLABS, 1, NX), F32), ((1, 12, 4, 32), BF16), ((1, 1, 3, 8), BF16))
    new_state, view, fine, coarse = pl.pallas_call(
        kernel,
        out_shape=tuple(pltpu.VMEM(*s) for s in shapes),
        in_specs=[any_space, pl.BlockSpec(memory_space=pltpu.SMEM)],
        out_specs=(vmem,) * 4,
        scratch_shapes=[
            pltpu.VMEM(state.shape, F32),
            pltpu.VMEM((NF * WZ, WX, NY), F32),
            pltpu.VMEM((NF, NZ, NX, NY), F32),
            pltpu.VMEM((NF * NZ, 24, NY), F32),
            pltpu.VMEM((NZ + 1, NF, NX, NY), F32),
                pltpu.VMEM((3, NF * NZ, NX, NY), F32),
            pltpu.VMEM((2, NY, NY), F32),
            pltpu.VMEM((2, NY, NY), F32),
            pltpu.VMEM((NY, NY), F32),
            pltpu.VMEM((2, 1, NY), F32),
            pltpu.VMEM((NF, NX, NY), F32),
            pltpu.VMEM((NF, NX, NY), F32),
            pltpu.VMEM((80, NY), F32),
            pltpu.VMEM((NX, NY), BF16),
            pltpu.VMEM((2, NF, 2, NX, NY), BF16),
            pltpu.VMEM((2, NF, 2, NZ, NY), BF16),
            pltpu.VMEM((NF, NX, NY), BF16),
            pltpu.VMEM((2, NF, 2, NX, NY), BF16),
            pltpu.VMEM((2, NF, 2, NZ, NY), BF16),
            pltpu.VMEM((2, NF, NX, NY), BF16),
            pltpu.VMEM((1, 1, NY), F32),
            pltpu.VMEM((N_NEAR - 1, 1, NY), F32),
            pltpu.VMEM((1, 1, NY), F32),
            pltpu.VMEM((N_NEAR - 1, 1, NY), F32),
            pltpu.VMEM((SLABS * N_GY, 1, NY), F32),
            pltpu.VMEM((SLABS, NX, NY), BF16),
            dma((CHUNKS,)), dma, dma((6,)), dma((6,)), dma((3,)), dma((3,)), dma, dma, dma, dma,
        ],
        compiler_params=pltpu.CompilerParams(collective_id=0, has_side_effects=True),
    )(state, view_dir)
    new_state, view, fine, coarse = pl.pallas_call(
        put_out,
        out_shape=tuple(jax.ShapeDtypeStruct(*s) for s in shapes),
        in_specs=[vmem] * 4,
        out_specs=(any_space,) * 4,
        scratch_shapes=[dma((4,))],
    )(*(pltpu.with_memory_space_constraint(a, pltpu.VMEM) for a in (new_state, view, fine, coarse)))
    return new_state, jnp.transpose(view, (0, 3, 1, 2)), fine, jnp.transpose(coarse, (0, 2, 1, 3))


def solution(mesh):
    in_specs = (P("grp", None, None, "gx", "gy"), P("gx"))
    out_specs = (
        P("grp", None, None, "gx", "gy"),
        P("grp", "gx", None, "gy"),
        P("grp", None, "gx", "gy"),
        P("grp", None, "gx", "gy"),
    )
    return jax.shard_map(body, mesh=mesh, in_specs=in_specs, out_specs=out_specs, check_vma=False)
```
